128 devices in a mesh: dev: 128 (over z, x, y, core).
Axes of the slice: x: 4, y: 4, z: 4, core: 2. Of those that a mesh axis runs over, the one named last changes fastest.
Arguments:
- cotangent: bfloat16 [32768, 2048], P('dev'), may hold values from -6 to 6
- hot_table: bfloat16 [2048, 128], replicated, may hold values from -6 to 6
- cold_table: float32 [262144, 128], P('dev'), may hold values from -6 to 6
- cold_m: float32 [262144, 128], P('dev'), may hold values from -0.75 to 0.75
- cold_v: float32 [262144, 128], P('dev'), may hold values from 0.0001 to 0.01
- cross_down: bfloat16 [2048, 512], replicated, may hold values from -0.125 to 0.125
- cross_up: bfloat16 [512, 2048], replicated, may hold values from -0.25 to 0.25
- cross_bias: float32 [2048], replicated, may hold values from -6 to 6
- dense_master: float32 [2048, 1024], P('dev'), may hold values from -0.4375 to 0.4375
- dense_m: float32 [2048, 1024], P('dev'), may hold values from -6 to 6
- dense_v: float32 [2048, 1024], P('dev'), may hold values from 1 to 30
- hot_ids: int32 [32768, 16], P('dev'), may hold values from 0 to 2047
- lookup_slot: int32 [32768, 16], P('dev'), may hold values from -1 to 3071, as said below
- fetch_rows: int32 [128, 128, 24], P('dev'), may hold values from 0 to 2047, as said below
Outputs:
- hot_grad: float32 [2048, 128], replicated
- bias_grad: float32 [2048], replicated
- cold_new: float32 [262144, 128], P('dev')
- cold_m_new: float32 [262144, 128], P('dev')
- cold_v_new: float32 [262144, 128], P('dev')
- master_new: float32 [2048, 1024], P('dev')
- dense_m_new: float32 [2048, 1024], P('dev')
- dense_v_new: float32 [2048, 1024], P('dev')
- new_weights: bfloat16 [2048, 1024], replicated
The draws below stay inside these ranges and needn't reach their ends.
Inputs may be any that keep to these rules, and one draw needn't show every extreme that they name: `lookup_slot`: -1 marks a hot lookup; any other value o * 24 + s reads slot s of the list that the lookup's device sends to owner o. For each device and owner the slots read are 0 to c - 1 for some c of at most 24, each read by exactly one lookup of that device; every device reads 24 slots from some owner, and some owner is read 24 slots by every device. `fetch_rows`: slots that no lookup reads still name rows.
All inputs are finite; a program needn't handle non-finite values.
Results may differ from the reference program's by a relative error of at most 0.0055.
Values may be sent and summed in bfloat16 or wider, within the bound.
A program may use at most 128 MiB of HBM per device.

```python
import math
import jax
import jax.numpy as jnp
from jax import lax

E = 128
F = 16
RANK = 512
HOT = 2048
SLAB = 2048
B_DEV = 256
CROSS = 2048
BATCH = 32768
MEAN_PAIR = 8
CAP = 24
COLD_ROWS = 262144
N_DEV = 128


def plan_counts(key):
    owner_order = jax.random.permutation(jax.random.fold_in(key, 11), N_DEV)
    owner_rank = jnp.zeros((N_DEV,), jnp.int32).at[owner_order].set(jnp.arange(N_DEV, dtype=jnp.int32))
    heavy_owner = owner_rank < N_DEV // 8
    heavy_counts = CAP - jax.random.randint(jax.random.fold_in(key, 12), (N_DEV, N_DEV), 0, MEAN_PAIR)
    light_counts = jax.random.randint(jax.random.fold_in(key, 13), (N_DEV, N_DEV), 0, 2 * MEAN_PAIR + 1)
    counts = jnp.where(heavy_owner[None, :], heavy_counts, light_counts).astype(jnp.int32)
    counts = counts.at[:, owner_order[0]].set(CAP)
    counts = counts.at[0, N_DEV - 1].set(CAP)
    return counts


def draw_lookup_slot(key, part):
    counts = plan_counts(key)
    lookups = B_DEV * F

    def one_device(device_counts, device_key):
        slot_ends = jnp.cumsum(device_counts).astype(jnp.int32)
        starts = slot_ends - device_counts
        places = jnp.arange(lookups, dtype=jnp.int32)
        owners = jnp.minimum(jnp.searchsorted(slot_ends, places, side='right'), N_DEV - 1).astype(jnp.int32)
        slot_index = places - starts[owners]
        slot_codes = jnp.where(places < slot_ends[-1], owners * CAP + slot_index, -1).astype(jnp.int32)
        shuffle = jax.random.permutation(device_key, lookups)
        return jnp.zeros((lookups,), jnp.int32).at[shuffle].set(slot_codes)
    device_keys = jax.random.split(jax.random.fold_in(key, 14), N_DEV)
    placed = jax.vmap(one_device)(counts, device_keys)
    return placed.reshape(N_DEV * B_DEV, F).astype(jnp.int32)


def draw_fetch_rows(key, part):
    return jax.random.randint(jax.random.fold_in(key, 15), (N_DEV, N_DEV, CAP), 0, SLAB).astype(jnp.int32)


def set_ends(drawn, stream_key, low, top_value):
    shape = drawn.shape
    place = [jax.random.randint(jax.random.fold_in(stream_key, axis), (), 0, shape[axis]) for axis in range(len(shape))]
    drawn = drawn.at[tuple(place)].set(low)
    longest = shape.index(max(shape))
    place[longest] = (place[longest] + 1) % shape[longest]
    return drawn.at[tuple(place)].set(top_value)


def level_of(rng, dims, cuts, least, high):
    factor_of = 1.0
    for axis_at, shards_of in cuts:
        draws = jax.random.uniform(jax.random.fold_in(jax.random.fold_in(rng, 6), axis_at), (shards_of,), jnp.float32, least / len(cuts), high / len(cuts))
        factor_of = factor_of * jnp.repeat(jnp.exp(draws), dims[axis_at] // shards_of).reshape((-1,) + (1,) * (len(dims) - 1 - axis_at))
    return factor_of


def centred(stream_key, dims, deviation, most, shards=(), kind=jnp.bfloat16):
    values = jax.random.normal(stream_key, dims, jnp.float32) * deviation
    if len(shards) > 0:
        values = level_of(stream_key, dims, shards, -0.22, 0.18) * values
    return jnp.clip(values, min=-most, max=most).astype(kind)


def setup_inputs(seed: int = 0) -> dict:
    key_list = jax.random.split(jax.random.key(seed), 15)
    cotangent = centred(key_list[0], (BATCH, CROSS), 1.0, 6.0, ((0, 128),))
    hot_table = centred(key_list[1], (HOT, E), 1.0, 6.0)
    cold_table = centred(key_list[2], (COLD_ROWS, E), 1.0, 6.0, ((0, 128),), jnp.float32)
    cold_m = centred(key_list[3], (COLD_ROWS, E), 0.05, 0.75, ((0, 128),), jnp.float32)
    cold_v = jnp.clip(jnp.exp(math.log(0.01) - 4.6051702 * jax.random.uniform(key_list[4], (COLD_ROWS, E), jnp.float32) ** level_of(key_list[4], (COLD_ROWS, E), ((0, 128),), -0.2, 0.2)), 0.0001, 0.01)
    cross_down = centred(key_list[5], (CROSS, RANK), CROSS ** -0.5, 0.125)
    cross_up = centred(key_list[6], (RANK, CROSS), RANK ** -0.5, 0.25)
    cross_bias = centred(key_list[7], (CROSS,), 0.5, 6.0, (), jnp.float32)
    dense_master = centred(key_list[8], (CROSS, 2 * RANK), 0.03, 0.4375, ((0, 128),), jnp.float32)
    dense_m = centred(key_list[9], (CROSS, 2 * RANK), 0.5, 6.0, ((0, 128),), jnp.float32)
    dense_v = jnp.clip(jnp.exp(math.log(30.0) - 3.4011974 * jax.random.uniform(key_list[10], (CROSS, 2 * RANK), jnp.float32) ** level_of(key_list[10], (CROSS, 2 * RANK), ((0, 128),), -0.2, 0.2)), 1.0, 30.0)
    hot_ids = set_ends(jax.random.randint(key_list[11], (BATCH, F), 0, HOT), jax.random.fold_in(key_list[11], 1), 0, HOT - 1).astype(jnp.int32)
    lookup_slot = draw_lookup_slot(jax.random.fold_in(key_list[14], 71), 0)
    fetch_rows = draw_fetch_rows(jax.random.fold_in(key_list[14], 71), 0)
    return dict(cotangent=cotangent, hot_table=hot_table, cold_table=cold_table, cold_m=cold_m, cold_v=cold_v, cross_down=cross_down, cross_up=cross_up, cross_bias=cross_bias, dense_master=dense_master, dense_m=dense_m, dense_v=dense_v, hot_ids=hot_ids, lookup_slot=lookup_slot, fetch_rows=fetch_rows)


first_decay = 0.9
second_decay = 0.999
adam_epsilon = 1e-08
learn_rate = 0.01
first_fix = 1.0 - (0.9 ** 10) ** 10
second_fix = 1.0 - (0.999 ** 10) ** 10

def adam_update(params, moment_one, moment_two, gradient):
    moment_one = first_decay * moment_one + (1.0 - first_decay) * gradient
    moment_two = second_decay * moment_two + (1.0 - second_decay) * gradient * gradient
    params = params - learn_rate * (moment_one / first_fix) / (jnp.sqrt(moment_two / second_fix) + adam_epsilon)
    return (params, moment_one, moment_two)

def reference(cotangent, hot_table, cold_table, cold_m, cold_v, cross_down, cross_up, cross_bias, dense_master, dense_m, dense_v, hot_ids, lookup_slot, fetch_rows):
    cold_half = cold_table.astype(jnp.bfloat16)
    owner_base = (jnp.arange(N_DEV, dtype=jnp.int32) * SLAB)[:, None]

    def per_device(totals, requester):
        hot_sum, bias_sum, dense_sum, cold_sum = totals
        first_row = (requester * B_DEV).astype(jnp.int32)
        grad_out = lax.dynamic_slice_in_dim(cotangent, first_row, B_DEV, 0)
        hot_index = lax.dynamic_slice_in_dim(hot_ids, first_row, B_DEV, 0)
        slot_code = lax.dynamic_slice_in_dim(lookup_slot, first_row, B_DEV, 0)
        requests = lax.dynamic_index_in_dim(fetch_rows, requester, 0, keepdims=False)
        global_rows = (owner_base + requests).reshape(-1).astype(jnp.int32)
        fetched = cold_half[global_rows]
        is_hot = slot_code < 0
        cold_pos = jnp.maximum(slot_code, 0)
        picked = jnp.where(is_hot[..., None], hot_table[hot_index], fetched[cold_pos])
        inputs = picked.reshape(B_DEV, CROSS)
        latent = jnp.dot(inputs, cross_down, preferred_element_type=jnp.float32).astype(jnp.bfloat16)
        mixing = jnp.dot(latent, cross_up, preferred_element_type=jnp.float32) + cross_bias
        grad_f32 = grad_out.astype(jnp.float32)
        grad_mix = (grad_f32 * inputs.astype(jnp.float32)).astype(jnp.bfloat16)
        grad_latent = jnp.dot(grad_mix, cross_up.T, preferred_element_type=jnp.float32).astype(jnp.bfloat16)
        grad_input = grad_f32 * (mixing + 1.0) + jnp.dot(grad_latent, cross_down.T, preferred_element_type=jnp.float32)
        per_lookup = grad_input.reshape(B_DEV * F, E)
        hot_target = jnp.where(is_hot, hot_index, HOT).reshape(-1)
        hot_sum = hot_sum.at[hot_target].add(per_lookup, mode='drop')
        cold_target = jnp.where(is_hot, COLD_ROWS, global_rows[cold_pos]).reshape(-1)
        cold_sum = cold_sum.at[cold_target].add(per_lookup, mode='drop')
        bias_sum = bias_sum + lax.optimization_barrier(jnp.sum(grad_mix.astype(jnp.float32), axis=0))
        down_part = jnp.dot(inputs.T, grad_latent, preferred_element_type=jnp.float32)
        up_part = jnp.dot(grad_mix.T, latent, preferred_element_type=jnp.float32)
        dense_sum = dense_sum + jnp.concatenate([down_part, up_part], axis=1)
        return ((hot_sum, bias_sum, dense_sum, cold_sum), None)
    start_totals = (jnp.zeros((HOT, E), jnp.float32), jnp.zeros((CROSS,), jnp.float32), jnp.zeros((CROSS, 2 * RANK), jnp.float32), jnp.zeros((COLD_ROWS, E), jnp.float32))
    totals, unused = lax.scan(per_device, start_totals, jnp.arange(N_DEV, dtype=jnp.int32))
    hot_sum, bias_sum, dense_sum, cold_sum = totals
    scale_mean = 1.0 / N_DEV
    hot_grad = hot_sum * scale_mean
    bias_grad = bias_sum * scale_mean
    cold_new, cold_m_new, cold_v_new = adam_update(cold_table, cold_m, cold_v, cold_sum * scale_mean)
    master_new, dense_m_new, dense_v_new = adam_update(dense_master, dense_m, dense_v, dense_sum * scale_mean)
    new_weights = master_new.astype(jnp.bfloat16)
    return (hot_grad, bias_grad, cold_new, cold_m_new, cold_v_new, master_new, dense_m_new, dense_v_new, new_weights)
```

```python
import jax
import jax.numpy as jnp
from jax import lax
from jax.experimental import pallas as pl
from jax.experimental.pallas import tpu as pltpu
from jax.sharding import PartitionSpec as P

MESH = pl.DeviceIdType.MESH

first_decay = 0.9
second_decay = 0.999
adam_epsilon = 1e-08
learn_rate = 0.01
first_fix = 1.0 - (0.9**10) ** 10
second_fix = 1.0 - (0.999**10) ** 10


def adam_update(params, moment_one, moment_two, gradient):
    moment_one = first_decay * moment_one + (1.0 - first_decay) * gradient
    moment_two = second_decay * moment_two + (1.0 - second_decay) * gradient * gradient
    params = params - learn_rate * (moment_one / first_fix) / (
        jnp.sqrt(moment_two / second_fix) + adam_epsilon
    )
    return (params, moment_one, moment_two)

CUTS = ((0, 384), (384, 768), (768, 1280))
ORDERS = ((0, 1, 2), (1, 2, 0), (2, 0, 1))


def coords_of(me):
    return [me // 32, lax.rem(me // 8, 4), lax.rem(me // 2, 4)], lax.rem(me, 2)


def device_of(place, core):
    return place[0] * 32 + place[1] * 8 + place[2] * 2 + core


def moved(place, axis, step):
    return [lax.rem(p + step, 4) if a == axis else p for a, p in enumerate(place)]


def reduce_kernel(part, master, m_in, v_in, out, master_out, m_out, v_out, *rest):
    first, sums0, got1, sums1, got2, sums2, got3 = (rest[3 * i : 3 * i + 3] for i in range(7))
    total, send_sem, recv_sem = rest[21:]
    place, core = coords_of(lax.axis_index("dev"))
    barrier = pltpu.get_barrier_semaphore()
    others = [device_of(place, 1 - core)]
    others += [device_of(moved(place, a, s), core) for a in range(3) for s in (1, 2, 3)]
    for other in others:
        pl.semaphore_signal(barrier, inc=1, device_id=(other,), device_id_type=MESH)
    pl.semaphore_wait(barrier, len(others))
    started = []

    def send(src, dst, color, phase, slot, other):
        copy = pltpu.make_async_remote_copy(
            src_ref=src,
            dst_ref=dst,
            send_sem=send_sem.at[color, phase, slot],
            recv_sem=recv_sem.at[color, phase, slot],
            device_id=(other,),
            device_id_type=MESH,
        )
        copy.start()
        started.append(copy)
        return copy

    waiting = {}
    for k, (low, high) in enumerate(CUTS):
        waiting[k] = [
            send(
                part.at[:, :, :, 1 - core, :, low:high],
                first[k],
                k,
                0,
                0,
                device_of(place, 1 - core),
            )
        ]
    for phase in range(4):
        for k, (low, high) in enumerate(CUTS):
            order = ORDERS[k]
            for copy in waiting[k]:
                copy.wait_recv()
            if phase == 0:

                def add_first(i, carry):
                    a = [i // 16, lax.rem(i // 4, 4), lax.rem(i, 4)]
                    zxy = [a[order.index(axis)] for axis in range(3)]
                    mine = part[zxy[0], zxy[1], zxy[2], core, :, low:high].astype(jnp.float32)
                    other = first[k][zxy[0], zxy[1], zxy[2]].astype(jnp.float32)
                    sums0[k][a[0], a[1], a[2]] = (mine + other).astype(jnp.bfloat16)
                    return carry

                lax.fori_loop(0, 64, add_first, 0)
            elif phase < 3:
                source = (sums0, sums1)[phase - 1][k].at[place[order[phase - 1]]]
                got = (got1, got2)[phase - 1][k]
                into = (sums1, sums2)[phase - 1][k]

                def add_more(i, carry):
                    at = (i // 4, lax.rem(i, 4)) if phase == 1 else (i,)
                    acc = source[at].astype(jnp.float32)
                    for slot in range(3):
                        acc = acc + got[(slot,) + at].astype(jnp.float32)
                    into[at] = acc.astype(jnp.bfloat16)
                    return carry

                lax.fori_loop(0, 16 if phase == 1 else 4, add_more, 0)
            else:
                acc = sums2[k][place[order[2]]].astype(jnp.float32)
                for slot in range(3):
                    acc = acc + got3[k][slot].astype(jnp.float32)
                total[:, low:high] = acc
            if phase < 3:
                axis = order[phase]
                source = (sums0, sums1, sums2)[phase][k]
                into = (got1, got2, got3)[phase][k]
                waiting[k] = [
                    send(
                        source.at[moved(place, axis, s)[axis]],
                        into.at[s - 1],
                        k,
                        1 + phase,
                        s - 1,
                        device_of(moved(place, axis, s), core),
                    )
                    for s in (1, 2, 3)
                ]
    scale = 1.0 / 128.0
    new, m_new, v_new = adam_update(master[...], m_in[...], v_in[...], total[:, :1024] * scale)
    master_out[...] = new
    m_out[...] = m_new
    v_out[...] = v_new
    out[place[0], place[1], place[2], core, :, :1024] = new.astype(jnp.bfloat16)
    out[place[0], place[1], place[2], core, :, 1024:] = (total[:, 1024:] * scale).astype(
        jnp.bfloat16
    )
    for phase in range(4):
        for k, (low, high) in enumerate(CUTS):
            order = ORDERS[k]
            for copy in waiting[k] if phase else []:
                copy.wait_recv()
            spread = order[3 - phase :]
            at = tuple(slice(None) if a in spread else place[a] for a in range(3))
            block = out.at[at + (core, slice(None), slice(low, high))]
            if phase < 3:
                axis = order[2 - phase]
                waiting[k] = [
                    send(
                        block, block, k, 4 + phase, s - 1, device_of(moved(place, axis, s), core)
                    )
                    for s in (1, 2, 3)
                ]
            else:
                waiting[k] = [send(block, block, k, 7, 0, device_of(place, 1 - core))]
    for k in range(3):
        for copy in waiting[k]:
            copy.wait_recv()
    for copy in started:
        copy.wait_send()


def reduce_all(part, master, m_in, v_in):
    widths = [high - low for low, high in CUTS]
    shapes = ((4, 4, 4), (4, 4, 4), (3, 4, 4), (4, 4), (3, 4), (4,), (3,))
    small = jax.ShapeDtypeStruct(master.shape, jnp.float32)
    vmem = pl.BlockSpec(memory_space=pltpu.VMEM)
    return pl.pallas_call(
        reduce_kernel,
        out_shape=(jax.ShapeDtypeStruct(part.shape, jnp.bfloat16), small, small, small),
        in_specs=[vmem] * 4,
        out_specs=(vmem,) * 4,
        scratch_shapes=[
            pltpu.VMEM(shape + (16, width), jnp.bfloat16) for shape in shapes for width in widths
        ]
        + [
            pltpu.VMEM((16, part.shape[-1]), jnp.float32),
            pltpu.SemaphoreType.DMA((3, 8, 3)),
            pltpu.SemaphoreType.DMA((3, 8, 3)),
        ],
        compiler_params=pltpu.CompilerParams(
            collective_id=0, has_side_effects=True, vmem_limit_bytes=48 * 2**20
        ),
        name="reduce_all",
    )(part, master, m_in, v_in)


def body(
    cotangent,
    hot_table,
    cold_table,
    cold_m,
    cold_v,
    cross_down,
    cross_up,
    cross_bias,
    dense_master,
    dense_m,
    dense_v,
    hot_ids,
    lookup_slot,
    fetch_rows,
):
    devices = lax.axis_size("dev")
    sample_count, fields = hot_ids.shape
    slab_rows, emb_width = cold_table.shape
    hot_rows = hot_table.shape[0]
    capacity = fetch_rows.shape[2]
    cross_width = cross_down.shape[0]
    shard_rows = dense_master.shape[0]
    scale_mean = 1.0 / devices
    requests = lax.all_to_all(fetch_rows, "dev", split_axis=1, concat_axis=0, tiled=True)
    request_flat = requests.reshape(devices * capacity)
    picked = jnp.take(cold_table, request_flat, axis=0).astype(jnp.bfloat16)
    fetched = lax.all_to_all(
        picked.reshape(devices, capacity, emb_width), "dev", split_axis=0, concat_axis=0, tiled=True
    )
    fetched_flat = fetched.reshape(devices * capacity, emb_width)
    is_hot = lookup_slot < 0
    cold_pos = jnp.maximum(lookup_slot, 0)
    chosen = jnp.where(
        is_hot[..., None],
        jnp.take(hot_table, hot_ids, axis=0),
        jnp.take(fetched_flat, cold_pos, axis=0),
    )
    inputs = chosen.reshape(sample_count, cross_width)
    latent = jnp.dot(inputs, cross_down, preferred_element_type=jnp.float32).astype(jnp.bfloat16)
    mixing = jnp.dot(latent, cross_up, preferred_element_type=jnp.float32) + cross_bias
    grad_f32 = cotangent.astype(jnp.float32)
    grad_mix = (grad_f32 * inputs.astype(jnp.float32)).astype(jnp.bfloat16)
    grad_latent = lax.dot_general(
        grad_mix, cross_up, (((1,), (1,)), ((), ())), preferred_element_type=jnp.float32
    ).astype(jnp.bfloat16)
    back_part = lax.dot_general(
        grad_latent, cross_down, (((1,), (1,)), ((), ())), preferred_element_type=jnp.float32
    )
    grad_input = grad_f32 * (mixing + 1.0) + back_part
    per_lookup = grad_input.reshape(sample_count * fields, emb_width)
    cold_target = jnp.where(is_hot, devices * capacity, lookup_slot).reshape(-1)
    cold_part = (
        jnp.zeros((devices * capacity, emb_width), jnp.float32)
        .at[cold_target]
        .add(per_lookup, mode="drop")
    )
    returned = lax.all_to_all(
        cold_part.reshape(devices, capacity, emb_width).astype(jnp.bfloat16),
        "dev",
        split_axis=0,
        concat_axis=0,
        tiled=True,
    ).astype(jnp.float32)
    cold_sum = (
        jnp.zeros((slab_rows, emb_width), jnp.float32)
        .at[request_flat]
        .add(returned.reshape(devices * capacity, emb_width))
    )
    cold_new, cold_m_new, cold_v_new = adam_update(
        cold_table, cold_m, cold_v, cold_sum * scale_mean
    )
    hot_target = jnp.where(is_hot, hot_ids, hot_rows).reshape(-1)
    hot_part = (
        jnp.zeros((hot_rows, emb_width), jnp.float32).at[hot_target].add(per_lookup, mode="drop")
    )
    bias_part = jnp.sum(grad_mix.astype(jnp.float32), axis=0)
    down_part = lax.dot_general(
        inputs, grad_latent, (((0,), (0,)), ((), ())), preferred_element_type=jnp.float32
    )
    up_part = lax.dot_general(
        grad_mix, latent, (((0,), (0,)), ((), ())), preferred_element_type=jnp.float32
    )
    column = jnp.pad(bias_part[:, None], ((0, 0), (0, emb_width - 1)))
    part = jnp.concatenate([down_part, up_part, hot_part, column], axis=1).astype(jnp.bfloat16)
    gathered, master_new, dense_m_new, dense_v_new = reduce_all(
        part.reshape(4, 4, 4, 2, shard_rows, part.shape[1]), dense_master, dense_m, dense_v
    )
    flat = gathered.reshape(part.shape)
    dense_cols = dense_master.shape[1]
    hot_grad = flat[:, dense_cols : dense_cols + emb_width].astype(jnp.float32)
    bias_grad = flat[:, dense_cols + emb_width].astype(jnp.float32)
    new_weights = flat[:, :dense_cols]
    return (
        hot_grad,
        bias_grad,
        cold_new,
        cold_m_new,
        cold_v_new,
        master_new,
        dense_m_new,
        dense_v_new,
        new_weights,
    )


def solution(mesh):
    return jax.shard_map(
        body,
        mesh=mesh,
        in_specs=(
            P("dev", None),
            P(),
            P("dev", None),
            P("dev", None),
            P("dev", None),
            P(),
            P(),
            P(),
            P("dev", None),
            P("dev", None),
            P("dev", None),
            P("dev", None),
            P("dev", None),
            P("dev", None, None),
        ),
        out_specs=(
            P(),
            P(),
            P("dev", None),
            P("dev", None),
            P("dev", None),
            P("dev", None),
            P("dev", None),
            P("dev", None),
            P(),
        ),
        check_vma=False,
    )
```

```python
import jax
import jax.numpy as jnp
from jax import lax
from jax.experimental import pallas as pl
from jax.experimental.pallas import tpu as pltpu
from jax.sharding import PartitionSpec as P

MESH = pl.DeviceIdType.MESH

first_decay = 0.9
second_decay = 0.999
adam_epsilon = 1e-08
learn_rate = 0.01
first_fix = 1.0 - (0.9**10) ** 10
second_fix = 1.0 - (0.999**10) ** 10


def adam_update(params, moment_one, moment_two, gradient):
    moment_one = first_decay * moment_one + (1.0 - first_decay) * gradient
    moment_two = second_decay * moment_two + (1.0 - second_decay) * gradient * gradient
    params = params - learn_rate * (moment_one / first_fix) / (
        jnp.sqrt(moment_two / second_fix) + adam_epsilon
    )
    return (params, moment_one, moment_two)

CUTS = ((0, 384), (384, 768), (768, 1280))
ORDERS = ((0, 1, 2), (1, 2, 0), (2, 0, 1))


def coords_of(me):
    return [me // 32, lax.rem(me // 8, 4), lax.rem(me // 2, 4)], lax.rem(me, 2)


def device_of(place, core):
    return place[0] * 32 + place[1] * 8 + place[2] * 2 + core


def moved(place, axis, step):
    return [lax.rem(p + step, 4) if a == axis else p for a, p in enumerate(place)]


def reduce_kernel(part, master, m_in, v_in, out, master_out, m_out, v_out, *rest):
    first, sums0, got1, sums1, got2, sums2, got3 = (rest[3 * i : 3 * i + 3] for i in range(7))
    total, send_sem, recv_sem = rest[21:]
    place, core = coords_of(lax.axis_index("dev"))
    barrier = pltpu.get_barrier_semaphore()
    others = [device_of(place, 1 - core)]
    others += [device_of(moved(place, a, s), core) for a in range(3) for s in (1, 2, 3)]
    for other in others:
        pl.semaphore_signal(barrier, inc=1, device_id=(other,), device_id_type=MESH)
    pl.semaphore_wait(barrier, len(others))
    started = []

    def send(src, dst, color, phase, slot, other):
        copy = pltpu.make_async_remote_copy(
            src_ref=src,
            dst_ref=dst,
            send_sem=send_sem.at[color, phase, slot],
            recv_sem=recv_sem.at[color, phase, slot],
            device_id=(other,),
            device_id_type=MESH,
        )
        copy.start()
        started.append(copy)
        return copy

    waiting = {}
    for k, (low, high) in enumerate(CUTS):
        waiting[k] = [
            send(
                part.at[:, :, :, 1 - core, :, low:high],
                first[k],
                k,
                0,
                0,
                device_of(place, 1 - core),
            )
        ]
    for phase in range(4):
        for k, (low, high) in enumerate(CUTS):
            order = ORDERS[k]
            for copy in waiting[k]:
                copy.wait_recv()
            if phase == 0:

                def add_first(i, carry):
                    a = [i // 16, lax.rem(i // 4, 4), lax.rem(i, 4)]
                    zxy = [a[order.index(axis)] for axis in range(3)]
                    mine = part[zxy[0], zxy[1], zxy[2], core, :, low:high].astype(jnp.float32)
                    other = first[k][zxy[0], zxy[1], zxy[2]].astype(jnp.float32)
                    sums0[k][a[0], a[1], a[2]] = (mine + other).astype(jnp.bfloat16)
                    return carry

                lax.fori_loop(0, 64, add_first, 0)
            elif phase < 3:
                source = (sums0, sums1)[phase - 1][k].at[place[order[phase - 1]]]
                got = (got1, got2)[phase - 1][k]
                into = (sums1, sums2)[phase - 1][k]

                def add_more(i, carry):
                    at = (i // 4, lax.rem(i, 4)) if phase == 1 else (i,)
                    acc = source[at].astype(jnp.float32)
                    for slot in range(3):
                        acc = acc + got[(slot,) + at].astype(jnp.float32)
                    into[at] = acc.astype(jnp.bfloat16)
                    return carry

                lax.fori_loop(0, 16 if phase == 1 else 4, add_more, 0)
            else:
                acc = sums2[k][place[order[2]]].astype(jnp.float32)
                for slot in range(3):
                    acc = acc + got3[k][slot].astype(jnp.float32)
                total[:, low:high] = acc
            if phase < 3:
                axis = order[phase]
                source = (sums0, sums1, sums2)[phase][k]
                into = (got1, got2, got3)[phase][k]
                waiting[k] = [
                    send(
                        source.at[moved(place, axis, s)[axis]],
                        into.at[s - 1],
                        k,
                        1 + phase,
                        s - 1,
                        device_of(moved(place, axis, s), core),
                    )
                    for s in (1, 2, 3)
                ]
    scale = 1.0 / 128.0
    new, m_new, v_new = adam_update(master[...], m_in[...], v_in[...], total[:, :1024] * scale)
    master_out[...] = new
    m_out[...] = m_new
    v_out[...] = v_new
    out[place[0], place[1], place[2], core, :, :1024] = new.astype(jnp.bfloat16)
    out[place[0], place[1], place[2], core, :, 1024:] = (total[:, 1024:] * scale).astype(
        jnp.bfloat16
    )
    for phase in range(4):
        for k, (low, high) in enumerate(CUTS):
            order = ORDERS[k]
            for copy in waiting[k] if phase else []:
                copy.wait_recv()
            spread = order[3 - phase :]
            at = tuple(slice(None) if a in spread else place[a] for a in range(3))
            block = out.at[at + (core, slice(None), slice(low, high))]
            if phase < 3:
                axis = order[2 - phase]
                waiting[k] = [
                    send(
                        block, block, k, 4 + phase, s - 1, device_of(moved(place, axis, s), core)
                    )
                    for s in (1, 2, 3)
                ]
            else:
                waiting[k] = [send(block, block, k, 7, 0, device_of(place, 1 - core))]
    for k in range(3):
        for copy in waiting[k]:
            copy.wait_recv()
    for copy in started:
        copy.wait_send()


def reduce_all(part, master, m_in, v_in):
    widths = [high - low for low, high in CUTS]
    shapes = ((4, 4, 4), (4, 4, 4), (3, 4, 4), (4, 4), (3, 4), (4,), (3,))
    small = jax.ShapeDtypeStruct(master.shape, jnp.float32)
    vmem = pl.BlockSpec(memory_space=pltpu.VMEM)
    return pl.pallas_call(
        reduce_kernel,
        out_shape=(jax.ShapeDtypeStruct(part.shape, jnp.bfloat16), small, small, small),
        in_specs=[vmem] * 4,
        out_specs=(vmem,) * 4,
        scratch_shapes=[
            pltpu.VMEM(shape + (16, width), jnp.bfloat16) for shape in shapes for width in widths
        ]
        + [
            pltpu.VMEM((16, part.shape[-1]), jnp.float32),
            pltpu.SemaphoreType.DMA((3, 8, 3)),
            pltpu.SemaphoreType.DMA((3, 8, 3)),
        ],
        compiler_params=pltpu.CompilerParams(
            collective_id=0, has_side_effects=True, vmem_limit_bytes=48 * 2**20
        ),
        name="reduce_all",
    )(part, master, m_in, v_in)

def peer_of(place, core, step):
    hops = (step // 32, lax.rem(step // 8, 4), lax.rem(step // 2, 4))
    there = [lax.rem(p + h, 4) for p, h in zip(place, hops)]
    return device_of(there, lax.rem(core + step, 2))


def fetch_kernel(
    lists, table, arrived, got, asked, picked, block, list_send, list_recv, row_send, row_recv, own_sem
):
    me = lax.axis_index("dev")
    place, core = coords_of(me)
    count, cap = picked.shape[:2]
    barrier = pltpu.get_barrier_semaphore()

    def greet(step, carry):
        other = peer_of(place, core, step)
        pl.semaphore_signal(barrier, inc=1, device_id=(other,), device_id_type=MESH)
        return carry

    lax.fori_loop(1, count, greet, 0)
    pl.semaphore_wait(barrier, count - 1)

    def list_copy(other):
        return pltpu.make_async_remote_copy(
            src_ref=lists.at[other],
            dst_ref=got.at[me],
            send_sem=list_send,
            recv_sem=list_recv,
            device_id=(other,),
            device_id_type=MESH,
        )

    def row_copy(other):
        return pltpu.make_async_remote_copy(
            src_ref=picked.at[other],
            dst_ref=arrived.at[me],
            send_sem=row_send,
            recv_sem=row_recv,
            device_id=(other,),
            device_id_type=MESH,
        )

    def all_of(source, target, send_sem, recv_sem):
        return pltpu.make_async_remote_copy(
            src_ref=source.at[pl.ds(0, count - 1)],
            dst_ref=target.at[pl.ds(0, count - 1)],
            send_sem=send_sem,
            recv_sem=recv_sem,
            device_id=(device_of(place, 1 - core),),
            device_id_type=MESH,
        )

    def send_list(step, carry):
        list_copy(peer_of(place, core, step)).start()
        return carry

    lax.fori_loop(1, count, send_list, 0)
    own = pltpu.make_async_copy(lists.at[me], got.at[me], own_sem)
    own.start()
    own.wait()
    all_lists = all_of(lists, got, list_send, list_recv)
    all_lists.wait_recv()
    read = pltpu.make_async_copy(got, asked, own_sem)
    read.start()
    read.wait()

    def pick(other):
        for j in range(cap):
            block[pl.ds(j, 1), :] = table[pl.ds(asked[other, 0, j], 1), :]
        return block[...].astype(jnp.bfloat16)

    def pick_send(step, carry):
        other = peer_of(place, core, step)
        picked[other] = pick(other)

        @pl.when(step > 1)
        def _():
            row_copy(peer_of(place, core, step - 1)).start()

        return carry

    lax.fori_loop(1, count, pick_send, 0)
    arrived[me] = pick(me)
    row_copy(peer_of(place, core, count - 1)).start()
    all_rows = all_of(picked, arrived, row_send, row_recv)
    all_rows.wait_recv()
    all_rows.wait_send()
    all_lists.wait_send()


def fetch_all(lists, table):
    count, cap = lists.shape
    emb = table.shape[1]
    vmem = pl.BlockSpec(memory_space=pltpu.VMEM)
    padded = jnp.pad(lists, ((0, 0), (0, emb - cap))).reshape(count, 1, emb)
    fetched, got = pl.pallas_call(
        fetch_kernel,
        out_shape=(
            jax.ShapeDtypeStruct((count, cap, emb), jnp.bfloat16),
            jax.ShapeDtypeStruct((count, 1, emb), jnp.int32),
        ),
        in_specs=[vmem] * 2,
        out_specs=(vmem, vmem),
        scratch_shapes=[
            pltpu.SMEM((count, 1, emb), jnp.int32),
            pltpu.VMEM((count, cap, emb), jnp.bfloat16),
            pltpu.VMEM((cap, emb), jnp.float32),
        ]
        + [pltpu.SemaphoreType.DMA(())] * 5,
        compiler_params=pltpu.CompilerParams(
            collective_id=1, has_side_effects=True, vmem_limit_bytes=24 * 2**20
        ),
        name="fetch_all",
    )(padded, table)
    return fetched, got[:, 0, :cap]


def cross_kernel(
    rows, ids, cot, hot, fetched, down, up, bias, part, cold, table, block, x_all, mix_all, grad, pair, slots
):
    samples, width = cot.shape
    hot_rows, emb = hot.shape
    owners, cap = fetched.shape[:2]
    fields = width // emb
    dense_cols = 2 * down.shape[1]
    f32, bf16 = jnp.float32, jnp.bfloat16

    def widen_hot(i, carry):
        at = pl.ds(pl.multiple_of(i * 256, 256), 256)
        table[at, :] = hot[at, :].astype(f32)
        return carry

    def widen_cold(i, carry):
        at = pl.ds(pl.multiple_of(hot_rows + i * cap, 8), cap)
        table[at, :] = fetched[i].astype(f32)
        return carry

    lax.fori_loop(0, hot_rows // 256, widen_hot, 0)
    lax.fori_loop(0, owners, widen_cold, 0)

    def gather_field(f, carry):
        cols = pl.ds(pl.multiple_of(f * emb, emb), emb)

        def gather_rows(i, inner):
            base = pl.multiple_of(i * 16, 16)
            for j in range(16):
                block[pl.ds(base + j, 1), :] = table[pl.ds(rows[f, base + j], 1), :]
            return inner

        lax.fori_loop(0, samples // 16, gather_rows, 0)
        x = block[...]
        x_all[:, cols] = x.astype(bf16)
        mix_all[:, cols] = (cot[:, cols].astype(f32) * x).astype(bf16)
        return carry

    lax.fori_loop(0, fields, gather_field, 0)
    nt = (((1,), (1,)), ((), ()))
    tn = (((0,), (0,)), ((), ()))
    latent = jnp.dot(x_all[...], down[...], preferred_element_type=f32).astype(bf16)
    back = lax.dot_general(mix_all[...], up[...], nt, preferred_element_type=f32).astype(bf16)
    ones = jnp.ones((samples, emb), bf16)
    latent_one = jnp.concatenate([latent, ones], axis=1)

    def per_chunk(n, carry):
        cols = pl.ds(pl.multiple_of(n * 256, 256), 256)
        mixing = jnp.dot(latent, up[:, cols], preferred_element_type=f32) + bias[:, cols]
        from_back = lax.dot_general(back, down[cols, :], nt, preferred_element_type=f32)
        g = cot[:, cols].astype(f32) * (mixing + 1.0) + from_back
        for h in range(2):
            at = pl.ds(pl.multiple_of((2 * n + h) * samples, samples), samples)
            piece = g[:, h * emb : (h + 1) * emb]
            grad[at, :] = piece
            high = piece.astype(bf16)
            pair[at, :emb] = high
            pair[at, emb:] = (piece - high.astype(f32)).astype(bf16)
        part[cols, : dense_cols // 2] = lax.dot_general(
            x_all[:, cols], back, tn, preferred_element_type=f32
        ).astype(bf16)
        up_part = lax.dot_general(
            mix_all[:, cols], latent_one, tn, preferred_element_type=f32
        ).astype(bf16)
        part[cols, dense_cols // 2 : dense_cols] = up_part[:, : dense_cols // 2]
        part[cols, dense_cols + emb :] = up_part[:, dense_cols // 2 :]
        return carry

    lax.fori_loop(0, width // 256, per_chunk, 0)
    slots[...] = jnp.zeros_like(slots)

    def place_field(f, carry):
        def place_rows(i, inner):
            base = pl.multiple_of(i * 16, 16)
            for j in range(16):
                row = rows[f, base + j]
                to = jnp.where(row >= hot_rows, row - hot_rows, owners * cap)
                slots[pl.ds(to, 1), :] = grad[pl.ds(f * samples + base + j, 1), :]
            return inner

        lax.fori_loop(0, samples // 16, place_rows, 0)
        return carry

    lax.fori_loop(0, fields, place_field, 0)

    def narrow(i, carry):
        cold[i] = slots[pl.ds(pl.multiple_of(i * cap, 8), cap), :].astype(bf16)
        return carry

    lax.fori_loop(0, owners, narrow, 0)

    def hot_tile(t, carry):
        first = pl.multiple_of(t * 256, 256)
        mine = first + lax.broadcasted_iota(jnp.int32, (256, samples), 0)
        acc = jnp.zeros((256, 2 * emb), f32)
        for f in range(fields):
            mask = jnp.where(mine == ids[f : f + 1, :], 1.0, 0.0).astype(bf16)
            acc = acc + jnp.dot(
                mask, pair[f * samples : (f + 1) * samples, :], preferred_element_type=f32
            )
        part[pl.ds(first, 256), dense_cols : dense_cols + emb] = (
            acc[:, :emb] + acc[:, emb:]
        ).astype(bf16)
        return carry

    lax.fori_loop(0, hot_rows // 256, hot_tile, 0)


def cross_layer(rows, ids, cot, hot, fetched, down, up, bias):
    samples, width = cot.shape
    hot_rows, emb = hot.shape
    owners, cap = fetched.shape[:2]
    vmem = pl.BlockSpec(memory_space=pltpu.VMEM)
    return pl.pallas_call(
        cross_kernel,
        out_shape=(
            jax.ShapeDtypeStruct((width, 2 * down.shape[1] + 2 * emb), jnp.bfloat16),
            jax.ShapeDtypeStruct((owners, cap, emb), jnp.bfloat16),
        ),
        in_specs=[pl.BlockSpec(memory_space=pltpu.SMEM)] + [vmem] * 7,
        out_specs=(vmem, vmem),
        scratch_shapes=[
            pltpu.VMEM((hot_rows + owners * cap, emb), jnp.float32),
            pltpu.VMEM((samples, emb), jnp.float32),
            pltpu.VMEM((samples, width), jnp.bfloat16),
            pltpu.VMEM((samples, width), jnp.bfloat16),
            pltpu.VMEM((samples * width // emb, emb), jnp.float32),
            pltpu.VMEM((samples * width // emb, 2 * emb), jnp.bfloat16),
            pltpu.VMEM((owners * cap + 8, emb), jnp.float32),
        ],
        compiler_params=pltpu.CompilerParams(vmem_limit_bytes=56 * 2**20),
        name="cross_layer",
    )(rows, ids, cot, hot, fetched, down, up, bias)


def body(
    cotangent,
    hot_table,
    cold_table,
    cold_m,
    cold_v,
    cross_down,
    cross_up,
    cross_bias,
    dense_master,
    dense_m,
    dense_v,
    hot_ids,
    lookup_slot,
    fetch_rows,
):
    devices = lax.axis_size("dev")
    slab_rows, emb_width = cold_table.shape
    hot_rows = hot_table.shape[0]
    capacity = fetch_rows.shape[2]
    cross_width = cross_down.shape[0]
    shard_rows = dense_master.shape[0]
    scale_mean = 1.0 / devices
    fetched, asked = fetch_all(fetch_rows[0], cold_table)
    request_flat = asked.reshape(devices * capacity)
    is_hot = lookup_slot < 0
    lookup_rows = jnp.where(is_hot, hot_ids, hot_rows + lookup_slot).T
    hot_only = jnp.where(is_hot, hot_ids, -1).T
    part, cold_part = cross_layer(
        lookup_rows,
        hot_only,
        cotangent,
        hot_table,
        fetched,
        cross_down,
        cross_up,
        cross_bias.reshape(1, cross_width),
    )
    returned = lax.all_to_all(
        cold_part,
        "dev",
        split_axis=0,
        concat_axis=0,
        tiled=True,
    ).astype(jnp.float32)
    cold_sum = (
        jnp.zeros((slab_rows, emb_width), jnp.float32)
        .at[request_flat]
        .add(returned.reshape(devices * capacity, emb_width))
    )
    cold_new, cold_m_new, cold_v_new = adam_update(
        cold_table, cold_m, cold_v, cold_sum * scale_mean
    )
    gathered, master_new, dense_m_new, dense_v_new = reduce_all(
        part.reshape(4, 4, 4, 2, shard_rows, part.shape[1]), dense_master, dense_m, dense_v
    )
    flat = gathered.reshape(part.shape)
    dense_cols = dense_master.shape[1]
    hot_grad = flat[:, dense_cols : dense_cols + emb_width].astype(jnp.float32)
    bias_grad = flat[:, dense_cols + emb_width].astype(jnp.float32)
    new_weights = flat[:, :dense_cols]
    return (
        hot_grad,
        bias_grad,
        cold_new,
        cold_m_new,
        cold_v_new,
        master_new,
        dense_m_new,
        dense_v_new,
        new_weights,
    )


def solution(mesh):
    return jax.shard_map(
        body,
        mesh=mesh,
        in_specs=(
            P("dev", None),
            P(),
            P("dev", None),
            P("dev", None),
            P("dev", None),
            P(),
            P(),
            P(),
            P("dev", None),
            P("dev", None),
            P("dev", None),
            P("dev", None),
            P("dev", None),
            P("dev", None, None),
        ),
        out_specs=(
            P(),
            P(),
            P("dev", None),
            P("dev", None),
            P("dev", None),
            P("dev", None),
            P("dev", None),
            P("dev", None),
            P(),
        ),
        check_vma=False,
    )
```

```python
import jax
import jax.numpy as jnp
from jax import lax
from jax.experimental import pallas as pl
from jax.experimental.pallas import tpu as pltpu
from jax.sharding import PartitionSpec as P

MESH = pl.DeviceIdType.MESH

first_decay = 0.9
second_decay = 0.999
adam_epsilon = 1e-08
learn_rate = 0.01
first_fix = 1.0 - (0.9**10) ** 10
second_fix = 1.0 - (0.999**10) ** 10


def adam_update(params, moment_one, moment_two, gradient):
    moment_one = first_decay * moment_one + (1.0 - first_decay) * gradient
    moment_two = second_decay * moment_two + (1.0 - second_decay) * gradient * gradient
    params = params - learn_rate * (moment_one / first_fix) / (
        jnp.sqrt(moment_two / second_fix) + adam_epsilon
    )
    return (params, moment_one, moment_two)

CUTS = ((0, 384), (384, 768), (768, 1152))
ORDERS = ((0, 1, 2), (1, 2, 0), (2, 0, 1))


def coords_of(me):
    return [me // 32, lax.rem(me // 8, 4), lax.rem(me // 2, 4)], lax.rem(me, 2)


def device_of(place, core):
    return place[0] * 32 + place[1] * 8 + place[2] * 2 + core


def moved(place, axis, step):
    return [lax.rem(p + step, 4) if a == axis else p for a, p in enumerate(place)]


def visit_peers(place, core, visit):
    tails = [lax.rem(place[2] + s, 4) * 2 + c for s in range(4) for c in (core, 1 - core)]

    def along_z(i, carry):
        z = lax.rem(place[0] + i, 4) * 32

        def along_x(j, inner):
            base = z + lax.rem(place[1] + j, 4) * 8
            visit([base + tail for tail in tails], i + j > 0)
            return inner

        return lax.fori_loop(0, 4, along_x, carry)

    lax.fori_loop(0, 4, along_z, 0)


def for_peers(place, core, act):
    def visit(others, away):
        pl.when(away)(lambda: act(others[0]))
        for other in others[1:]:
            act(other)

    visit_peers(place, core, visit)


def meet_all(place, core):
    barrier = pltpu.get_barrier_semaphore()
    for_peers(
        place,
        core,
        lambda other: pl.semaphore_signal(
            barrier, inc=1, device_id=(other,), device_id_type=MESH
        ),
    )
    pl.semaphore_wait(barrier, 127)


def remote(source, target, send_sem, recv_sem, other):
    return pltpu.make_async_remote_copy(
        src_ref=source,
        dst_ref=target,
        send_sem=send_sem,
        recv_sem=recv_sem,
        device_id=(other,),
        device_id_type=MESH,
    )


def fetch_kernel(
    lists, table, arrived, got, asked, picked, block, list_send, list_recv, row_send, row_recv, own_sem
):
    me = lax.axis_index("dev")
    place, core = coords_of(me)
    partner = device_of(place, 1 - core)
    count, cap = picked.shape[:2]
    most = pl.ds(0, count - 1)
    meet_all(place, core)
    for_peers(
        place,
        core,
        lambda other: remote(lists.at[other], got.at[me], list_send, list_recv, other).start(),
    )
    own = pltpu.make_async_copy(lists.at[me], got.at[me], own_sem)
    own.start()
    own.wait()
    all_lists = remote(lists.at[most], got.at[most], list_send, list_recv, partner)
    all_lists.wait_recv()
    read = pltpu.make_async_copy(got, asked, own_sem)
    read.start()
    read.wait()

    def pick(other, k):
        for j in range(cap):
            block[k, pl.ds(j, 1), :] = table[pl.ds(asked[other, 0, j], 1), :]
        picked[other] = block[k].astype(jnp.bfloat16)

    def send(other):
        remote(picked.at[other], arrived.at[me], row_send, row_recv, other).start()

    def visit(others, away):
        for k, other in enumerate(others):
            pick(other, k)
        pl.when(away)(lambda: send(others[0]))
        for other in others[1:]:
            send(other)

    visit_peers(place, core, visit)
    arrived[me] = picked[me]
    all_rows = remote(picked.at[most], arrived.at[most], row_send, row_recv, partner)
    all_rows.wait_recv()
    all_rows.wait_send()
    all_lists.wait_send()


def fetch_all(lists, table):
    count, cap = lists.shape
    emb = table.shape[1]
    vmem = pl.BlockSpec(memory_space=pltpu.VMEM)
    padded = jnp.pad(lists, ((0, 0), (0, emb - cap))).reshape(count, 1, emb)
    fetched, got = pl.pallas_call(
        fetch_kernel,
        out_shape=(
            jax.ShapeDtypeStruct((count, cap, emb), jnp.bfloat16),
            jax.ShapeDtypeStruct((count, 1, emb), jnp.int32),
        ),
        in_specs=[vmem] * 2,
        out_specs=(vmem, vmem),
        scratch_shapes=[
            pltpu.SMEM((count, 1, emb), jnp.int32),
            pltpu.VMEM((count, cap, emb), jnp.bfloat16),
            pltpu.VMEM((8, cap, emb), jnp.float32),
        ]
        + [pltpu.SemaphoreType.DMA(())] * 5,
        compiler_params=pltpu.CompilerParams(
            collective_id=1, has_side_effects=True, vmem_limit_bytes=24 * 2**20
        ),
        name="fetch_all",
    )(padded, table)
    return fetched, got[:, 0, :cap]


def reduce_kernel(
    part,
    bias,
    master,
    m_in,
    v_in,
    cold,
    slots,
    cold_table,
    cold_m,
    cold_v,
    out,
    bias_out,
    master_out,
    m_out,
    v_out,
    cold_out,
    cold_m_out,
    cold_v_out,
    *rest,
):
    first, sums0, got1, sums1, got2, sums2, got3 = (rest[3 * i : 3 * i + 3] for i in range(7))
    total, bias_sum, bias_got, returned, wide, flat = rest[21:27]
    send_sem, recv_sem, cold_send, cold_recv, own_sem = rest[27:]
    me = lax.axis_index("dev")
    place, core = coords_of(me)
    partner = device_of(place, 1 - core)
    count, cap, emb = cold.shape
    dense = master.shape[1]
    scale = 1.0 / count
    f32, bf16 = jnp.float32, jnp.bfloat16
    meet_all(place, core)
    started = []

    def send(src, dst, color, phase, slot, other):
        copy = remote(
            src, dst, send_sem.at[color, phase, slot], recv_sem.at[color, phase, slot], other
        )
        copy.start()
        started.append(copy)
        return copy

    def slab(axis, at, free):
        return tuple(at if a == axis else slice(None) for a in free)

    waiting = {}
    for k, (low, high) in enumerate(CUTS):
        waiting[k] = [
            send(part.at[:, :, :, 1 - core, :, low:high], first[k], k, 0, 0, partner)
        ]
    waiting[3] = [send(bias, bias_got.at[0, 0], 3, 0, 0, partner)]
    for_peers(
        place,
        core,
        lambda other: remote(cold.at[other], returned.at[me], cold_send, cold_recv, other).start(),
    )
    own = pltpu.make_async_copy(cold.at[me], returned.at[me], own_sem)
    own.start()
    own.wait()
    for phase in range(4):
        for k, (low, high) in enumerate(CUTS):
            axis = ORDERS[k][phase] if phase < 3 else None
            free = [a for a in range(3) if a not in ORDERS[k][: phase - 1]] if phase else None
            for copy in waiting[k]:
                copy.wait_recv()
            if phase == 0:

                def add_first(i, carry):
                    for x in range(4):
                        mine = part[i, x, :, core, :, low:high].astype(f32)
                        sums0[k][i, x] = (mine + first[k][i, x].astype(f32)).astype(bf16)
                    return carry

                lax.fori_loop(0, 4, add_first, 0)
            else:
                before = ORDERS[k][phase - 1]
                source = (sums0, sums1, sums2)[phase - 1][k]
                got = (got1, got2, got3)[phase - 1][k]
                mine = source[slab(before, place[before], free)].astype(f32)
                for slot in range(3):
                    mine = mine + got[slot].astype(f32)
                if phase < 3:
                    (sums1, sums2)[phase - 1][k][...] = mine.astype(bf16)
                else:
                    total[:, low:high] = mine
            if phase < 3:
                source = (sums0, sums1, sums2)[phase][k]
                into = (got1, got2, got3)[phase][k]
                left = [a for a in range(3) if a not in ORDERS[k][:phase]]
                waiting[k] = [
                    send(
                        source.at[slab(axis, moved(place, axis, s)[axis], left)],
                        into.at[s - 1],
                        k,
                        1 + phase,
                        s - 1,
                        device_of(moved(place, axis, s), core),
                    )
                    for s in (1, 2, 3)
                ]
        for copy in waiting[3]:
            copy.wait_recv()
        if phase == 0:
            bias_sum[0] = bias[...] + bias_got[0, 0]
        else:
            bias_sum[phase] = (bias_sum[phase - 1] + bias_got[phase, 0]) + (
                bias_got[phase, 1] + bias_got[phase, 2]
            )
        if phase < 3:
            waiting[3] = [
                send(
                    bias_sum.at[phase],
                    bias_got.at[phase + 1, s - 1],
                    3,
                    1 + phase,
                    s - 1,
                    device_of(moved(place, phase, s), core),
                )
                for s in (1, 2, 3)
            ]
    bias_out[...] = bias_sum[3] * scale
    new, m_new, v_new = adam_update(master[...], m_in[...], v_in[...], total[:, :dense] * scale)
    master_out[...] = new
    m_out[...] = m_new
    v_out[...] = v_new
    out[place[0], place[1], place[2], core, :, :dense] = new.astype(bf16)
    out[place[0], place[1], place[2], core, :, dense:] = (total[:, dense:] * scale).astype(bf16)

    def update_cold():
        most = pl.ds(0, count - 1)
        all_cold = remote(cold.at[most], returned.at[most], cold_send, cold_recv, partner)
        all_cold.wait_recv()

        def widen(i, carry):
            wide[pl.ds(pl.multiple_of(i * cap, 8), cap), :] = returned[i].astype(f32)
            return carry

        lax.fori_loop(0, count, widen, 0)
        flat[...] = wide[...].astype(bf16)

        def update_tile(t, carry):
            at = pl.ds(pl.multiple_of(t * 256, 256), 256)
            mine = t * 256 + lax.broadcasted_iota(jnp.int32, (256, 512), 0)
            acc = jnp.zeros((256, emb), f32)
            for c in range(count * cap // 512):
                mask = jnp.where(mine == slots[:, c * 512 : (c + 1) * 512], 1.0, 0.0).astype(bf16)
                acc = acc + jnp.dot(
                    mask, flat[c * 512 : (c + 1) * 512, :], preferred_element_type=f32
                )
            new, m_new, v_new = adam_update(
                cold_table[at, :], cold_m[at, :], cold_v[at, :], acc * scale
            )
            cold_out[at, :] = new
            cold_m_out[at, :] = m_new
            cold_v_out[at, :] = v_new
            return carry

        lax.fori_loop(0, cold_table.shape[0] // 256, update_tile, 0)
        all_cold.wait_send()

    for phase in range(4):
        for k, (low, high) in enumerate(CUTS):
            order = ORDERS[k]
            for copy in waiting[k] if phase else []:
                copy.wait_recv()
            spread = order[3 - phase :]
            at = tuple(slice(None) if a in spread else place[a] for a in range(3))
            block = out.at[at + (core, slice(None), slice(low, high))]
            if phase < 3:
                axis = order[2 - phase]
                waiting[k] = [
                    send(
                        block, block, k, 4 + phase, s - 1, device_of(moved(place, axis, s), core)
                    )
                    for s in (1, 2, 3)
                ]
            else:
                waiting[k] = [send(block, block, k, 7, 0, partner)]
        if phase == 2:
            update_cold()
    for k in range(3):
        for copy in waiting[k]:
            copy.wait_recv()
    for copy in started:
        copy.wait_send()


def reduce_all(part, bias, master, m_in, v_in, cold, slots, cold_table, cold_m, cold_v):
    widths = [high - low for low, high in CUTS]
    shapes = ((4, 4, 4), (4, 4, 4), (3, 4, 4), (4, 4), (3, 4), (4,), (3,))
    small = jax.ShapeDtypeStruct(master.shape, jnp.float32)
    slab = jax.ShapeDtypeStruct(cold_table.shape, jnp.float32)
    vmem = pl.BlockSpec(memory_space=pltpu.VMEM)
    count, cap, emb = cold.shape
    return pl.pallas_call(
        reduce_kernel,
        out_shape=(
            jax.ShapeDtypeStruct(part.shape, jnp.bfloat16),
            jax.ShapeDtypeStruct(bias.shape, jnp.float32),
        )
        + (small,) * 3
        + (slab,) * 3,
        in_specs=[vmem] * 10,
        out_specs=(vmem,) * 8,
        scratch_shapes=[
            pltpu.VMEM(shape + (16, width), jnp.bfloat16) for shape in shapes for width in widths
        ]
        + [
            pltpu.VMEM((16, part.shape[-1]), jnp.float32),
            pltpu.VMEM((4,) + bias.shape, jnp.float32),
            pltpu.VMEM((4, 3) + bias.shape, jnp.float32),
            pltpu.VMEM(cold.shape, jnp.bfloat16),
            pltpu.VMEM((count * cap, emb), jnp.float32),
            pltpu.VMEM((count * cap, emb), jnp.bfloat16),
            pltpu.SemaphoreType.DMA((4, 8, 3)),
            pltpu.SemaphoreType.DMA((4, 8, 3)),
        ]
        + [pltpu.SemaphoreType.DMA(())] * 3,
        compiler_params=pltpu.CompilerParams(
            collective_id=0, has_side_effects=True, vmem_limit_bytes=48 * 2**20
        ),
        name="reduce_all",
    )(part, bias, master, m_in, v_in, cold, slots, cold_table, cold_m, cold_v)


def cross_kernel(
    rows, puts, ids, cot, hot, fetched, down, up, bias, part, bias_part, cold, table, block, x_all, mix_all, grad, pair, slots
):
    samples, width = cot.shape
    hot_rows, emb = hot.shape
    owners, cap = fetched.shape[:2]
    fields = width // emb
    dense_cols = 2 * down.shape[1]
    f32, bf16 = jnp.float32, jnp.bfloat16

    def widen_hot(i, carry):
        at = pl.ds(pl.multiple_of(i * 256, 256), 256)
        table[at, :] = hot[at, :].astype(f32)
        return carry

    def widen_cold(i, carry):
        at = pl.ds(pl.multiple_of(hot_rows + i * cap, 8), cap)
        table[at, :] = fetched[i].astype(f32)
        return carry

    lax.fori_loop(0, hot_rows // 256, widen_hot, 0)
    lax.fori_loop(0, owners, widen_cold, 0)

    def gather_field(f, carry):
        cols = pl.ds(pl.multiple_of(f * emb, emb), emb)

        def gather_rows(i, inner):
            base = pl.multiple_of(i * 16, 16)
            first = f * samples + base
            for j in range(16):
                block[pl.ds(base + j, 1), :] = table[pl.ds(rows[first + j], 1), :]
            return inner

        lax.fori_loop(0, samples // 16, gather_rows, 0)
        x = block[...]
        x_all[:, cols] = x.astype(bf16)
        mix_all[:, cols] = (cot[:, cols].astype(f32) * x).astype(bf16)
        return carry

    lax.fori_loop(0, fields, gather_field, 0)
    nt = (((1,), (1,)), ((), ()))
    tn = (((0,), (0,)), ((), ()))
    latent = jnp.dot(x_all[...], down[...], preferred_element_type=f32).astype(bf16)
    back = lax.dot_general(mix_all[...], up[...], nt, preferred_element_type=f32).astype(bf16)
    ones = jnp.ones((8, samples), bf16)

    def per_chunk(n, carry):
        cols = pl.ds(pl.multiple_of(n * 256, 256), 256)
        mixing = jnp.dot(latent, up[:, cols], preferred_element_type=f32) + bias[:, cols]
        from_back = lax.dot_general(back, down[cols, :], nt, preferred_element_type=f32)
        g = cot[:, cols].astype(f32) * (mixing + 1.0) + from_back
        for h in range(2):
            at = pl.ds(pl.multiple_of((2 * n + h) * samples, samples), samples)
            piece = g[:, h * emb : (h + 1) * emb]
            grad[at, :] = piece
            high = piece.astype(bf16)
            pair[at, :emb] = high
            pair[at, emb:] = (piece - high.astype(f32)).astype(bf16)
        part[cols, : dense_cols // 2] = lax.dot_general(
            x_all[:, cols], back, tn, preferred_element_type=f32
        ).astype(bf16)
        part[cols, dense_cols // 2 : dense_cols] = lax.dot_general(
            mix_all[:, cols], latent, tn, preferred_element_type=f32
        ).astype(bf16)
        bias_part[:, cols] = jnp.dot(ones, mix_all[:, cols], preferred_element_type=f32)[:1]
        return carry

    lax.fori_loop(0, width // 256, per_chunk, 0)
    slots[...] = jnp.zeros_like(slots)

    def place_rows(i, carry):
        base = pl.multiple_of(i * 16, 16)
        for j in range(16):
            slots[pl.ds(puts[base + j], 1), :] = grad[pl.ds(base + j, 1), :]
        return carry

    lax.fori_loop(0, fields * samples // 16, place_rows, 0)

    def narrow(i, carry):
        cold[i] = slots[pl.ds(pl.multiple_of(i * cap, 8), cap), :].astype(bf16)
        return carry

    lax.fori_loop(0, owners, narrow, 0)

    def hot_tile(t, carry):
        first = pl.multiple_of(t * 256, 256)
        mine = first + lax.broadcasted_iota(jnp.int32, (256, samples), 0)
        acc = jnp.zeros((256, 2 * emb), f32)
        for f in range(fields):
            mask = jnp.where(mine == ids[f : f + 1, :], 1.0, 0.0).astype(bf16)
            acc = acc + jnp.dot(
                mask, pair[f * samples : (f + 1) * samples, :], preferred_element_type=f32
            )
        part[pl.ds(first, 256), dense_cols : dense_cols + emb] = (
            acc[:, :emb] + acc[:, emb:]
        ).astype(bf16)
        return carry

    lax.fori_loop(0, hot_rows // 256, hot_tile, 0)


def cross_layer(rows, puts, ids, cot, hot, fetched, down, up, bias):
    samples, width = cot.shape
    hot_rows, emb = hot.shape
    owners, cap = fetched.shape[:2]
    vmem = pl.BlockSpec(memory_space=pltpu.VMEM)
    return pl.pallas_call(
        cross_kernel,
        out_shape=(
            jax.ShapeDtypeStruct((width, 2 * down.shape[1] + emb), jnp.bfloat16),
            jax.ShapeDtypeStruct((1, width), jnp.float32),
            jax.ShapeDtypeStruct((owners, cap, emb), jnp.bfloat16),
        ),
        in_specs=[pl.BlockSpec(memory_space=pltpu.SMEM)] * 2 + [vmem] * 7,
        out_specs=(vmem,) * 3,
        scratch_shapes=[
            pltpu.VMEM((hot_rows + owners * cap, emb), jnp.float32),
            pltpu.VMEM((samples, emb), jnp.float32),
            pltpu.VMEM((samples, width), jnp.bfloat16),
            pltpu.VMEM((samples, width), jnp.bfloat16),
            pltpu.VMEM((samples * width // emb, emb), jnp.float32),
            pltpu.VMEM((samples * width // emb, 2 * emb), jnp.bfloat16),
            pltpu.VMEM((owners * cap + 8, emb), jnp.float32),
        ],
        compiler_params=pltpu.CompilerParams(vmem_limit_bytes=56 * 2**20),
        name="cross_layer",
    )(rows, puts, ids, cot, hot, fetched, down, up, bias)


def body(
    cotangent,
    hot_table,
    cold_table,
    cold_m,
    cold_v,
    cross_down,
    cross_up,
    cross_bias,
    dense_master,
    dense_m,
    dense_v,
    hot_ids,
    lookup_slot,
    fetch_rows,
):
    devices = lax.axis_size("dev")
    hot_rows = hot_table.shape[0]
    capacity = fetch_rows.shape[2]
    cross_width = cross_down.shape[0]
    shard_rows = dense_master.shape[0]
    fetched, asked = fetch_all(fetch_rows[0], cold_table)
    is_hot = lookup_slot < 0
    lookup_rows = jnp.where(is_hot, hot_ids, hot_rows + lookup_slot).T.reshape(-1)
    put_rows = jnp.where(is_hot, devices * capacity, lookup_slot).T.reshape(-1)
    hot_only = jnp.where(is_hot, hot_ids, -1).T
    part, bias_part, cold_part = cross_layer(
        lookup_rows,
        put_rows,
        hot_only,
        cotangent,
        hot_table,
        fetched,
        cross_down,
        cross_up,
        cross_bias.reshape(1, cross_width),
    )
    gathered, bias_grad, master_new, dense_m_new, dense_v_new, cold_new, cold_m_new, cold_v_new = reduce_all(
        part.reshape(4, 4, 4, 2, shard_rows, part.shape[1]),
        bias_part,
        dense_master,
        dense_m,
        dense_v,
        cold_part,
        asked.reshape(1, devices * capacity),
        cold_table,
        cold_m,
        cold_v,
    )
    flat = gathered.reshape(part.shape)
    dense_cols = dense_master.shape[1]
    hot_grad = flat[:, dense_cols:].astype(jnp.float32)
    bias_grad = bias_grad.reshape(cross_width)
    new_weights = flat[:, :dense_cols]
    return (
        hot_grad,
        bias_grad,
        cold_new,
        cold_m_new,
        cold_v_new,
        master_new,
        dense_m_new,
        dense_v_new,
        new_weights,
    )


def solution(mesh):
    return jax.shard_map(
        body,
        mesh=mesh,
        in_specs=(
            P("dev", None),
            P(),
            P("dev", None),
            P("dev", None),
            P("dev", None),
            P(),
            P(),
            P(),
            P("dev", None),
            P("dev", None),
            P("dev", None),
            P("dev", None),
            P("dev", None),
            P("dev", None, None),
        ),
        out_specs=(
            P(),
            P(),
            P("dev", None),
            P("dev", None),
            P("dev", None),
            P("dev", None),
            P("dev", None),
            P("dev", None),
            P(),
        ),
        check_vma=False,
    )
```

```python
import jax
import jax.numpy as jnp
from jax import lax
from jax.experimental import pallas as pl
from jax.experimental.pallas import tpu as pltpu
from jax.sharding import PartitionSpec as P

MESH = pl.DeviceIdType.MESH

first_decay = 0.9
second_decay = 0.999
adam_epsilon = 1e-08
learn_rate = 0.01
first_fix = 1.0 - (0.9**10) ** 10
second_fix = 1.0 - (0.999**10) ** 10


def adam_update(params, moment_one, moment_two, gradient):
    moment_one = first_decay * moment_one + (1.0 - first_decay) * gradient
    moment_two = second_decay * moment_two + (1.0 - second_decay) * gradient * gradient
    params = params - learn_rate * (moment_one / first_fix) / (
        jnp.sqrt(moment_two / second_fix) + adam_epsilon
    )
    return (params, moment_one, moment_two)

CUTS = ((0, 384), (384, 768), (768, 1152))
ORDERS = ((0, 1, 2), (1, 2, 0), (2, 0, 1))


def coords_of(me):
    return [me // 32, lax.rem(me // 8, 4), lax.rem(me // 2, 4)], lax.rem(me, 2)


def device_of(place, core):
    return place[0] * 32 + place[1] * 8 + place[2] * 2 + core


def moved(place, axis, step):
    return [lax.rem(p + step, 4) if a == axis else p for a, p in enumerate(place)]


def visit_peers(place, core, visit):
    tails = [lax.rem(place[2] + s, 4) * 2 + c for s in range(4) for c in (core, 1 - core)]

    def along_z(i, carry):
        z = lax.rem(place[0] + i, 4) * 32

        def along_x(j, inner):
            base = z + lax.rem(place[1] + j, 4) * 8
            visit([base + tail for tail in tails], i + j > 0)
            return inner

        return lax.fori_loop(0, 4, along_x, carry)

    lax.fori_loop(0, 4, along_z, 0)


def for_peers(place, core, act):
    def visit(others, away):
        pl.when(away)(lambda: act(others[0]))
        for other in others[1:]:
            act(other)

    visit_peers(place, core, visit)


def remote(source, target, send_sem, recv_sem, other):
    return pltpu.make_async_remote_copy(
        src_ref=source,
        dst_ref=target,
        send_sem=send_sem,
        recv_sem=recv_sem,
        device_id=(other,),
        device_id_type=MESH,
    )


def step_kernel(
    rows,
    lists,
    puts,
    ids,
    hot,
    cold_table,
    bias,
    master,
    m_in,
    v_in,
    cot_far,
    down_far,
    up_far,
    cold_m_far,
    cold_v_far,
    out,
    bias_out,
    master_out,
    m_out,
    v_out,
    cold_out,
    cold_m_out,
    cold_v_out,
    *rest,
):
    first, sums0, got1, sums1, got2, sums2, got3 = (rest[3 * i : 3 * i + 3] for i in range(7))
    cot, down, up, cold_m, cold_v, asked, inverse = rest[21:28]
    got, picked, arrived, block, spread_rows, inverse_row = rest[28:34]
    table, x_all, mix_all, grad, pair, part, bias_part = rest[34:41]
    cold, returned, wide, flat, total, bias_sum, bias_got = rest[41:48]
    send_sem, recv_sem, load_sem = rest[48:51]
    list_send, list_recv, row_send, row_recv, cold_send, cold_recv, own_sem = rest[51:]
    f32, bf16 = jnp.float32, jnp.bfloat16
    me = lax.axis_index("dev")
    place, core = coords_of(me)
    partner = device_of(place, 1 - core)
    samples, width = cot.shape
    hot_rows, emb = hot.shape
    count, cap = picked.shape[:2]
    fields = width // emb
    half = down.shape[1]
    dense = 2 * half
    scale = 1.0 / count
    most = pl.ds(0, count - 1)
    nt = (((1,), (1,)), ((), ()))
    tn = (((0,), (0,)), ((), ()))

    barrier = pltpu.get_barrier_semaphore()
    for_peers(
        place,
        core,
        lambda other: pl.semaphore_signal(
            barrier, inc=1, device_id=(other,), device_id_type=MESH
        ),
    )
    loads = [
        pltpu.make_async_copy(far, near, load_sem.at[i])
        for i, (far, near) in enumerate(
            (
                (cot_far, cot),
                (down_far, down),
                (up_far, up),
                (cold_m_far, cold_m),
                (cold_v_far, cold_v),
            )
        )
    ]
    for load in loads:
        load.start()

    which = lax.broadcasted_iota(jnp.int32, (8, samples), 0)
    sample = lax.broadcasted_iota(jnp.int32, (8, samples), 1).astype(f32)

    def invert(t, carry):
        mine = t * 256 + lax.broadcasted_iota(jnp.int32, (256, samples), 0)
        acc = jnp.zeros((8, 256), f32)
        for f in range(fields):
            mask = jnp.where(mine == puts[f : f + 1, :], 1.0, 0.0).astype(bf16)
            code = jnp.where(which == 0, f + 1.0, sample).astype(bf16)
            acc = acc + lax.dot_general(code, mask, nt, preferred_element_type=f32)
        found = ((acc[0:1] - 1.0) * samples + acc[1:2]).astype(jnp.int32)
        inverse_row[:, pl.ds(pl.multiple_of(t * 256, 256), 256)] = jnp.where(
            acc[0:1] > 0.5, jnp.clip(found, 0, fields * samples), fields * samples
        )
        return carry

    lax.fori_loop(0, count * cap // 256, invert, 0)
    pl.semaphore_wait(barrier, count - 1)

    for_peers(
        place,
        core,
        lambda other: remote(lists.at[other], got.at[me], list_send, list_recv, other).start(),
    )
    own = pltpu.make_async_copy(lists.at[me], got.at[me], own_sem)
    own.start()
    own.wait()
    own = pltpu.make_async_copy(inverse_row, inverse, own_sem)
    own.start()
    own.wait()

    def widen_hot(i, carry):
        at = pl.ds(pl.multiple_of(i * 256, 256), 256)
        table[at, :] = hot[at, :].astype(f32)
        return carry

    lax.fori_loop(0, hot_rows // 256, widen_hot, 0)
    all_lists = remote(lists.at[most], got.at[most], list_send, list_recv, partner)
    all_lists.wait_recv()
    read = pltpu.make_async_copy(got, asked, own_sem)
    read.start()
    read.wait()

    def exchange(pick, source, target, sends, receives):
        def send(other):
            remote(source.at[other], target.at[me], sends, receives, other).start()

        def visit(others, away):
            for k, other in enumerate(others):
                pick(other, k)
            pl.when(away)(lambda: send(others[0]))
            for other in others[1:]:
                send(other)

        visit_peers(place, core, visit)
        target[me] = source[me]
        return remote(source.at[most], target.at[most], sends, receives, partner)

    def pick_row(other, k):
        for j in range(cap):
            block[k, pl.ds(j, 1), :] = cold_table[pl.ds(asked[other, 0, j], 1), :]
        picked[other] = block[k].astype(bf16)

    all_rows = exchange(pick_row, picked, arrived, row_send, row_recv)
    turned = got[:, 0, :].astype(f32).T.astype(jnp.int32)
    for j in range(cap):
        spread_rows[:, j * count : (j + 1) * count] = turned[j : j + 1, :]
    grad[pl.ds(fields * samples, 8), :] = jnp.zeros((8, emb), f32)
    for load in loads[:3]:
        load.wait()
    all_rows.wait_recv()

    def widen_cold(i, carry):
        at = pl.ds(pl.multiple_of(hot_rows + i * cap, 8), cap)
        table[at, :] = arrived[i].astype(f32)
        return carry

    lax.fori_loop(0, count, widen_cold, 0)

    def gather_field(f, carry):
        cols = pl.ds(pl.multiple_of(f * emb, emb), emb)

        def gather_rows(i, inner):
            base = pl.multiple_of(f * samples + i * 16, 16)
            for j in range(16):
                grad[pl.ds(base + j, 1), :] = table[pl.ds(rows[base + j], 1), :]
            return inner

        lax.fori_loop(0, samples // 16, gather_rows, 0)
        x = grad[pl.ds(pl.multiple_of(f * samples, samples), samples), :]
        x_all[:, cols] = x.astype(bf16)
        mix_all[:, cols] = (cot[:, cols].astype(f32) * x).astype(bf16)
        return carry

    lax.fori_loop(0, fields, gather_field, 0)
    latent = jnp.dot(x_all[...], down[...], preferred_element_type=f32).astype(bf16)
    back = lax.dot_general(mix_all[...], up[...], nt, preferred_element_type=f32).astype(bf16)
    ones = jnp.ones((8, samples), bf16)

    def per_chunk(n, carry):
        cols = pl.ds(pl.multiple_of(n * 256, 256), 256)
        mixing = jnp.dot(latent, up[:, cols], preferred_element_type=f32) + bias[:, cols]
        from_back = lax.dot_general(back, down[cols, :], nt, preferred_element_type=f32)
        g = cot[:, cols].astype(f32) * (mixing + 1.0) + from_back
        for h in range(2):
            at = pl.ds(pl.multiple_of((2 * n + h) * samples, samples), samples)
            piece = g[:, h * emb : (h + 1) * emb]
            grad[at, :] = piece
            high = piece.astype(bf16)
            pair[at, :emb] = high
            pair[at, emb:] = (piece - high.astype(f32)).astype(bf16)
        z, x = n // 2, pl.ds(lax.rem(n, 2) * 2, 2)
        down_part = lax.dot_general(x_all[:, cols], back, tn, preferred_element_type=f32)
        up_part = lax.dot_general(mix_all[:, cols], latent, tn, preferred_element_type=f32)
        part[z, x, :, :, :, :half] = down_part.astype(bf16).reshape(2, 4, 2, 16, half)
        part[z, x, :, :, :, half:dense] = up_part.astype(bf16).reshape(2, 4, 2, 16, half)
        bias_part[:, cols] = jnp.dot(ones, mix_all[:, cols], preferred_element_type=f32)[:1]
        return carry

    lax.fori_loop(0, width // 256, per_chunk, 0)
    started = []

    def send(src, dst, color, phase, slot, other):
        copy = remote(
            src, dst, send_sem.at[color, phase, slot], recv_sem.at[color, phase, slot], other
        )
        copy.start()
        started.append(copy)
        return copy

    def slab(axis, at, free):
        return tuple(at if a == axis else slice(None) for a in free)

    waiting = {}

    def swap_cores(k):
        low, high = CUTS[k]
        waiting[k] = [
            send(part.at[:, :, :, 1 - core, :, low:high], first[k], k, 0, 0, partner)
        ]

    def collect(k, phase):
        low, high = CUTS[k]
        for copy in waiting[k]:
            copy.wait_recv()
        if phase == 0:

            def add_first(i, carry):
                for x in range(4):
                    mine = part[i, x, :, core, :, low:high].astype(f32)
                    sums0[k][i, x] = (mine + first[k][i, x].astype(f32)).astype(bf16)
                return carry

            lax.fori_loop(0, 4, add_first, 0)
        else:
            before = ORDERS[k][phase - 1]
            free = [a for a in range(3) if a not in ORDERS[k][: phase - 1]]
            source = (sums0, sums1, sums2)[phase - 1][k]
            arrivals = (got1, got2, got3)[phase - 1][k]
            mine = source[slab(before, place[before], free)].astype(f32)
            for slot in range(3):
                mine = mine + arrivals[slot].astype(f32)
            if phase < 3:
                (sums1, sums2)[phase - 1][k][...] = mine.astype(bf16)
            else:
                total[:, low:high] = mine
        if phase < 3:
            axis = ORDERS[k][phase]
            left = [a for a in range(3) if a not in ORDERS[k][:phase]]
            waiting[k] = [
                send(
                    (sums0, sums1, sums2)[phase][k].at[
                        slab(axis, moved(place, axis, s)[axis], left)
                    ],
                    (got1, got2, got3)[phase][k].at[s - 1],
                    k,
                    1 + phase,
                    s - 1,
                    device_of(moved(place, axis, s), core),
                )
                for s in (1, 2, 3)
            ]

    def collect_bias(phase):
        for copy in waiting[3]:
            copy.wait_recv()
        if phase == 0:
            bias_sum[0] = bias_part[...] + bias_got[0, 0]
        else:
            bias_sum[phase] = (bias_sum[phase - 1] + bias_got[phase, 0]) + (
                bias_got[phase, 1] + bias_got[phase, 2]
            )
        if phase < 3:
            waiting[3] = [
                send(
                    bias_sum.at[phase],
                    bias_got.at[phase + 1, s - 1],
                    3,
                    1 + phase,
                    s - 1,
                    device_of(moved(place, phase, s), core),
                )
                for s in (1, 2, 3)
            ]

    swap_cores(0)
    swap_cores(1)
    waiting[3] = [send(bias_part, bias_got.at[0, 0], 3, 0, 0, partner)]

    def pick_grad(other, k):
        base = other * cap
        for j in range(cap):
            block[k, pl.ds(j, 1), :] = grad[pl.ds(inverse[0, base + j], 1), :]
        cold[other] = block[k].astype(bf16)

    all_cold = exchange(pick_grad, cold, returned, cold_send, cold_recv)
    collect(0, 0)
    collect(1, 0)

    def hot_tile(t, carry):
        mine = t * 256 + lax.broadcasted_iota(jnp.int32, (256, samples), 0)
        acc = jnp.zeros((256, 2 * emb), f32)
        for f in range(fields):
            mask = jnp.where(mine == ids[f : f + 1, :], 1.0, 0.0).astype(bf16)
            acc = acc + jnp.dot(
                mask, pair[f * samples : (f + 1) * samples, :], preferred_element_type=f32
            )
        both = (acc[:, :emb] + acc[:, emb:]).astype(bf16)
        x = pl.ds(lax.rem(t, 2) * 2, 2)
        part[t // 2, x, :, :, :, dense:] = both.reshape(2, 4, 2, 16, emb)
        return carry

    lax.fori_loop(0, hot_rows // 256, hot_tile, 0)
    swap_cores(2)
    collect_bias(0)
    collect(2, 0)
    for phase in (1, 2, 3):
        for k in range(3):
            collect(k, phase)
        collect_bias(phase)
    bias_out[...] = bias_sum[3] * scale
    new, m_new, v_new = adam_update(master[...], m_in[...], v_in[...], total[:, :dense] * scale)
    master_out[...] = new
    m_out[...] = m_new
    v_out[...] = v_new
    out[place[0], place[1], place[2], core, :, :dense] = new.astype(bf16)
    out[place[0], place[1], place[2], core, :, dense:] = (total[:, dense:] * scale).astype(bf16)

    def update_cold():
        for load in loads[3:]:
            load.wait()
        all_cold.wait_recv()

        def widen(i, carry):
            wide[pl.ds(pl.multiple_of(i * cap, 8), cap), :] = returned[i].astype(f32)
            return carry

        lax.fori_loop(0, count, widen, 0)
        for j in range(cap):
            flat[j * count : (j + 1) * count, :] = wide[pl.ds(j, count, stride=cap), :].astype(
                bf16
            )

        def update_tile(t, carry):
            at = pl.ds(pl.multiple_of(t * 256, 256), 256)
            mine = t * 256 + lax.broadcasted_iota(jnp.int32, (256, 512), 0)
            acc = jnp.zeros((256, emb), f32)
            for c in range(count * cap // 512):
                cut = slice(c * 512, (c + 1) * 512)
                mask = jnp.where(mine == spread_rows[:, cut], 1.0, 0.0).astype(bf16)
                acc = acc + jnp.dot(mask, flat[cut, :], preferred_element_type=f32)
            new, m_new, v_new = adam_update(
                cold_table[at, :], cold_m[at, :], cold_v[at, :], acc * scale
            )
            cold_out[at, :] = new
            cold_m_out[at, :] = m_new
            cold_v_out[at, :] = v_new
            return carry

        lax.fori_loop(0, cold_table.shape[0] // 256, update_tile, 0)

    for phase in range(4):
        for k, (low, high) in enumerate(CUTS):
            order = ORDERS[k]
            for copy in waiting[k] if phase else []:
                copy.wait_recv()
            spread = order[3 - phase :]
            at = tuple(slice(None) if a in spread else place[a] for a in range(3))
            region = out.at[at + (core, slice(None), slice(low, high))]
            if phase < 3:
                axis = order[2 - phase]
                waiting[k] = [
                    send(
                        region, region, k, 4 + phase, s - 1, device_of(moved(place, axis, s), core)
                    )
                    for s in (1, 2, 3)
                ]
            else:
                waiting[k] = [send(region, region, k, 7, 0, partner)]
        if phase == 2:
            update_cold()
    for k in range(3):
        for copy in waiting[k]:
            copy.wait_recv()
    for copy in started:
        copy.wait_send()
    for everything in (all_lists, all_rows, all_cold):
        everything.wait_send()


def step_all(rows, lists, puts, ids, hot, cold_table, bias, dense_state, cot, down, up, cold_m, cold_v):
    f32, bf16, i32 = jnp.float32, jnp.bfloat16, jnp.int32
    count, cap = lists.shape
    hot_rows, emb = hot.shape
    samples, width = cot.shape
    lookups = samples * width // emb
    total_cols = 2 * down.shape[1] + emb
    widths = [high - low for low, high in CUTS]
    shapes = ((4, 4, 4), (4, 4, 4), (3, 4, 4), (4, 4), (3, 4), (4,), (3,))
    small = jax.ShapeDtypeStruct(dense_state[0].shape, f32)
    slab = jax.ShapeDtypeStruct(cold_table.shape, f32)
    vmem = pl.BlockSpec(memory_space=pltpu.VMEM)
    padded = jnp.pad(lists, ((0, 0), (0, emb - cap))).reshape(count, 1, emb)
    return pl.pallas_call(
        step_kernel,
        out_shape=(
            jax.ShapeDtypeStruct((4, 4, 4, 2, 16, total_cols), bf16),
            jax.ShapeDtypeStruct(bias.shape, f32),
        )
        + (small,) * 3
        + (slab,) * 3,
        in_specs=[pl.BlockSpec(memory_space=pltpu.SMEM)]
        + [vmem] * 9
        + [pl.BlockSpec(memory_space=pl.ANY)] * 5,
        out_specs=(vmem,) * 8,
        scratch_shapes=[
            pltpu.VMEM(shape + (16, cols), bf16) for shape in shapes for cols in widths
        ]
        + [
            pltpu.VMEM(cot.shape, bf16),
            pltpu.VMEM(down.shape, bf16),
            pltpu.VMEM(up.shape, bf16),
            pltpu.VMEM(cold_m.shape, f32),
            pltpu.VMEM(cold_v.shape, f32),
            pltpu.SMEM((count, 1, emb), i32),
            pltpu.SMEM((1, count * cap), i32),
            pltpu.VMEM((count, 1, emb), i32),
            pltpu.VMEM((count, cap, emb), bf16),
            pltpu.VMEM((count, cap, emb), bf16),
            pltpu.VMEM((8, cap, emb), f32),
            pltpu.VMEM((1, count * cap), i32),
            pltpu.VMEM((1, count * cap), i32),
            pltpu.VMEM((hot_rows + count * cap, emb), f32),
            pltpu.VMEM((samples, width), bf16),
            pltpu.VMEM((samples, width), bf16),
            pltpu.VMEM((lookups + 8, emb), f32),
            pltpu.VMEM((lookups, 2 * emb), bf16),
            pltpu.VMEM((4, 4, 4, 2, 16, total_cols), bf16),
            pltpu.VMEM(bias.shape, f32),
            pltpu.VMEM((count, cap, emb), bf16),
            pltpu.VMEM((count, cap, emb), bf16),
            pltpu.VMEM((count * cap + cap, emb), f32),
            pltpu.VMEM((count * cap, emb), bf16),
            pltpu.VMEM((16, total_cols), f32),
            pltpu.VMEM((4,) + bias.shape, f32),
            pltpu.VMEM((4, 3) + bias.shape, f32),
            pltpu.SemaphoreType.DMA((4, 8, 3)),
            pltpu.SemaphoreType.DMA((4, 8, 3)),
            pltpu.SemaphoreType.DMA((5,)),
        ]
        + [pltpu.SemaphoreType.DMA(())] * 7,
        compiler_params=pltpu.CompilerParams(
            collective_id=0, has_side_effects=True, vmem_limit_bytes=60 * 2**20
        ),
        name="step_all",
    )(rows, padded, puts, ids, hot, cold_table, bias, *dense_state, cot, down, up, cold_m, cold_v)


def body(
    cotangent,
    hot_table,
    cold_table,
    cold_m,
    cold_v,
    cross_down,
    cross_up,
    cross_bias,
    dense_master,
    dense_m,
    dense_v,
    hot_ids,
    lookup_slot,
    fetch_rows,
):
    hot_rows = hot_table.shape[0]
    cross_width = cross_down.shape[0]
    is_hot = lookup_slot < 0
    lookup_rows = jnp.where(is_hot, hot_ids, hot_rows + lookup_slot).T.reshape(-1)
    hot_only = jnp.where(is_hot, hot_ids, -1).T
    gathered, bias_grad, master_new, dense_m_new, dense_v_new, cold_new, cold_m_new, cold_v_new = step_all(
        lookup_rows,
        fetch_rows[0],
        lookup_slot.T,
        hot_only,
        hot_table,
        cold_table,
        cross_bias.reshape(1, cross_width),
        (dense_master, dense_m, dense_v),
        cotangent,
        cross_down,
        cross_up,
        cold_m,
        cold_v,
    )
    flat = gathered.reshape(cross_width, -1)
    dense_cols = dense_master.shape[1]
    hot_grad = flat[:, dense_cols:].astype(jnp.float32)
    bias_grad = bias_grad.reshape(cross_width)
    new_weights = flat[:, :dense_cols]
    return (
        hot_grad,
        bias_grad,
        cold_new,
        cold_m_new,
        cold_v_new,
        master_new,
        dense_m_new,
        dense_v_new,
        new_weights,
    )


def solution(mesh):
    return jax.shard_map(
        body,
        mesh=mesh,
        in_specs=(
            P("dev", None),
            P(),
            P("dev", None),
            P("dev", None),
            P("dev", None),
            P(),
            P(),
            P(),
            P("dev", None),
            P("dev", None),
            P("dev", None),
            P("dev", None),
            P("dev", None),
            P("dev", None, None),
        ),
        out_specs=(
            P(),
            P(),
            P("dev", None),
            P("dev", None),
            P("dev", None),
            P("dev", None),
            P("dev", None),
            P("dev", None),
            P(),
        ),
        check_vma=False,
    )
```

```python
import jax
import jax.numpy as jnp
from jax import lax
from jax.experimental import pallas as pl
from jax.experimental.pallas import tpu as pltpu
from jax.sharding import PartitionSpec as P

MESH = pl.DeviceIdType.MESH

first_decay = 0.9
second_decay = 0.999
adam_epsilon = 1e-08
learn_rate = 0.01
first_fix = 1.0 - (0.9**10) ** 10
second_fix = 1.0 - (0.999**10) ** 10


def adam_update(params, moment_one, moment_two, gradient):
    moment_one = first_decay * moment_one + (1.0 - first_decay) * gradient
    moment_two = second_decay * moment_two + (1.0 - second_decay) * gradient * gradient
    params = params - learn_rate * (moment_one / first_fix) / (
        jnp.sqrt(moment_two / second_fix) + adam_epsilon
    )
    return (params, moment_one, moment_two)

CUTS = ((0, 384), (384, 768), (768, 1024), (1024, 1152))
ORDERS = ((0, 1, 2), (1, 2, 0), (2, 0, 1), (2, 0, 1))
COLORS = len(CUTS)
BIAS = COLORS


def coords_of(me):
    return [me // 32, lax.rem(me // 8, 4), lax.rem(me // 2, 4)], lax.rem(me, 2)


def device_of(place, core):
    return place[0] * 32 + place[1] * 8 + place[2] * 2 + core


def moved(place, axis, step):
    return [lax.rem(p + step, 4) if a == axis else p for a, p in enumerate(place)]


def visit_peers(place, core, visit):
    tails = [lax.rem(place[2] + s, 4) * 2 + c for s in range(4) for c in (core, 1 - core)]

    def along_z(i, carry):
        z = lax.rem(place[0] + i, 4) * 32

        def along_x(j, inner):
            base = z + lax.rem(place[1] + j, 4) * 8
            visit([base + tail for tail in tails], i + j > 0)
            return inner

        return lax.fori_loop(0, 4, along_x, carry)

    lax.fori_loop(0, 4, along_z, 0)


def for_peers(place, core, act):
    def visit(others, away):
        pl.when(away)(lambda: act(others[0]))
        for other in others[1:]:
            act(other)

    visit_peers(place, core, visit)


def remote(source, target, send_sem, recv_sem, other):
    return pltpu.make_async_remote_copy(
        src_ref=source,
        dst_ref=target,
        send_sem=send_sem,
        recv_sem=recv_sem,
        device_id=(other,),
        device_id_type=MESH,
    )


def step_kernel(
    rows,
    lists,
    puts,
    ids,
    hot,
    cold_table,
    bias,
    master,
    m_in,
    v_in,
    cot_far,
    down_far,
    up_far,
    cold_m_far,
    cold_v_far,
    out,
    bias_out,
    total_out,
    cold_out,
    cold_m_out,
    cold_v_out,
    *rest,
):
    first, sums0, got1, sums1, got2, sums2, got3 = (
        rest[COLORS * i : COLORS * i + COLORS] for i in range(7)
    )
    rest = rest[COLORS * 7 - 21 :]
    cot, down, up, cold_m, cold_v, asked, inverse = rest[21:28]
    got, picked, arrived, block, spread_rows, inverse_row = rest[28:34]
    table, x_all, mix_all, grad, pair, part, bias_part = rest[34:41]
    cold, returned, wide, flat, total, bias_sum, bias_got = rest[41:48]
    mid = rest[58]
    stage_send, stage_recv, far_sem = rest[59:]
    send_sem, recv_sem, load_sem = rest[48:51]
    list_send, list_recv, row_send, row_recv, cold_send, cold_recv, own_sem = rest[51:58]
    f32, bf16 = jnp.float32, jnp.bfloat16
    me = lax.axis_index("dev")
    place, core = coords_of(me)
    partner = device_of(place, 1 - core)
    samples, width = cot.shape
    hot_rows, emb = hot.shape
    count, cap = picked.shape[:2]
    fields = width // emb
    half = down.shape[1]
    dense = 2 * half
    scale = 1.0 / count
    most = pl.ds(0, count - 1)
    nt = (((1,), (1,)), ((), ()))
    tn = (((0,), (0,)), ((), ()))

    plane, spot = place[0] * 4 + place[1], place[2] * 2 + core
    planes = [
        lax.rem(place[0] + i, 4) * 4 + lax.rem(place[1] + j, 4)
        for i in range(4)
        for j in range(4)
        if i + j > 0
    ]
    spots = [
        lax.rem(place[2] + i, 4) * 2 + c
        for i in range(4)
        for c in (core, 1 - core)
    ][1:]
    barrier = pltpu.get_barrier_semaphore()
    greeted = [other * 8 + spot for other in planes] + [plane * 8 + other for other in spots]
    for other in greeted:
        pl.semaphore_signal(barrier, inc=1, device_id=(other,), device_id_type=MESH)
    loads = [
        pltpu.make_async_copy(far, near, load_sem.at[i])
        for i, (far, near) in enumerate(
            (
                (cot_far, cot),
                (down_far, down),
                (up_far, up),
                (cold_m_far, cold_m),
                (cold_v_far, cold_v),
            )
        )
    ]
    for load in loads:
        load.start()

    which = lax.broadcasted_iota(jnp.int32, (8, samples), 0)
    sample = lax.broadcasted_iota(jnp.int32, (8, samples), 1).astype(f32)

    def invert(t, carry):
        mine = t * 256 + lax.broadcasted_iota(jnp.int32, (256, samples), 0)
        acc = jnp.zeros((8, 256), f32)
        for f in range(fields):
            mask = jnp.where(mine == puts[f : f + 1, :], 1.0, 0.0).astype(bf16)
            code = jnp.where(which == 0, f + 1.0, sample).astype(bf16)
            acc = acc + lax.dot_general(code, mask, nt, preferred_element_type=f32)
        found = ((acc[0:1] - 1.0) * samples + acc[1:2]).astype(jnp.int32)
        inverse_row[:, pl.ds(pl.multiple_of(t * 256, 256), 256)] = jnp.where(
            acc[0:1] > 0.5, jnp.clip(found, 0, fields * samples), fields * samples
        )
        return carry

    mid[plane] = lists[plane]
    lax.fori_loop(0, count * cap // 256, invert, 0)
    keep = pltpu.make_async_copy(inverse_row, inverse, own_sem)
    keep.start()
    pl.semaphore_wait(barrier, len(greeted))
    for other in planes:
        remote(lists.at[other], mid.at[plane], list_send, list_recv, other * 8 + spot).start()

    def widen_hot(i, carry):
        at = pl.ds(pl.multiple_of(i * 256, 256), 256)
        table[at, :] = hot[at, :].astype(f32)
        return carry

    lax.fori_loop(0, hot_rows // 256, widen_hot, 0)
    part_of = pl.ds(0, len(planes))
    all_lists = remote(lists.at[part_of], mid.at[part_of], list_send, list_recv, partner)
    all_lists.wait_recv()
    for other in spots:
        remote(
            mid.at[:, other], got.at[:, spot], stage_send, stage_recv, plane * 8 + other
        ).start()
    got[:, spot] = mid[:, spot]
    part_of = pl.ds(0, len(spots))
    all_stage = remote(mid.at[:, part_of], got.at[:, part_of], stage_send, stage_recv, partner)
    all_stage.wait_recv()
    read = pltpu.make_async_copy(got, asked, far_sem)
    read.start()
    read.wait()

    def exchange(pick, source, target, sends, receives):
        def send(other):
            remote(source.at[other], target.at[me], sends, receives, other).start()

        def visit(others, away):
            for k, other in enumerate(others):
                pick(other, k)
            pl.when(away)(lambda: send(others[0]))
            for other in others[1:]:
                send(other)

        visit_peers(place, core, visit)
        target[me] = source[me]
        return remote(source.at[most], target.at[most], sends, receives, partner)

    def pick_row(other, k):
        for j in range(cap):
            block[k, pl.ds(j, 1), :] = cold_table[pl.ds(asked[other // 8, lax.rem(other, 8), 0, j], 1), :]
        picked[other] = block[k].astype(bf16)

    all_rows = exchange(pick_row, picked, arrived, row_send, row_recv)
    turned = got[:, :, 0, :].reshape(count, emb).astype(f32).T.astype(jnp.int32)
    for j in range(cap):
        spread_rows[:, j * count : (j + 1) * count] = turned[j : j + 1, :]
    grad[pl.ds(fields * samples, 8), :] = jnp.zeros((8, emb), f32)
    for load in loads[:3]:
        load.wait()
    all_rows.wait_recv()

    def widen_cold(i, carry):
        at = pl.ds(pl.multiple_of(hot_rows + i * cap, 8), cap)
        table[at, :] = arrived[i].astype(f32)
        return carry

    lax.fori_loop(0, count, widen_cold, 0)

    def gather_field(f, carry):
        cols = pl.ds(pl.multiple_of(f * emb, emb), emb)

        def gather_rows(i, inner):
            base = pl.multiple_of(f * samples + i * 16, 16)
            for j in range(16):
                grad[pl.ds(base + j, 1), :] = table[pl.ds(rows[base + j], 1), :]
            return inner

        lax.fori_loop(0, samples // 16, gather_rows, 0)
        x = grad[pl.ds(pl.multiple_of(f * samples, samples), samples), :]
        x_all[:, cols] = x.astype(bf16)
        mix_all[:, cols] = (cot[:, cols].astype(f32) * x).astype(bf16)
        return carry

    lax.fori_loop(0, fields, gather_field, 0)
    latent = jnp.dot(x_all[...], down[...], preferred_element_type=f32).astype(bf16)
    back = lax.dot_general(mix_all[...], up[...], nt, preferred_element_type=f32).astype(bf16)
    ones = jnp.ones((8, samples), bf16)

    def weight_chunk(n, carry):
        cols = pl.ds(pl.multiple_of(n * 256, 256), 256)
        z, x = n // 2, pl.ds(lax.rem(n, 2) * 2, 2)
        down_part = lax.dot_general(x_all[:, cols], back, tn, preferred_element_type=f32)
        up_part = lax.dot_general(mix_all[:, cols], latent, tn, preferred_element_type=f32)
        part[z, x, :, :, :, :half] = down_part.astype(bf16).reshape(2, 4, 2, 16, half)
        part[z, x, :, :, :, half:dense] = up_part.astype(bf16).reshape(2, 4, 2, 16, half)
        bias_part[:, cols] = jnp.dot(ones, mix_all[:, cols], preferred_element_type=f32)[:1]
        return carry

    def grad_chunk(n, carry):
        cols = pl.ds(pl.multiple_of(n * 256, 256), 256)
        mixing = jnp.dot(latent, up[:, cols], preferred_element_type=f32) + bias[:, cols]
        from_back = lax.dot_general(back, down[cols, :], nt, preferred_element_type=f32)
        g = cot[:, cols].astype(f32) * (mixing + 1.0) + from_back
        for h in range(2):
            at = pl.ds(pl.multiple_of((2 * n + h) * samples, samples), samples)
            piece = g[:, h * emb : (h + 1) * emb]
            grad[at, :] = piece
            high = piece.astype(bf16)
            pair[at, :emb] = high
            pair[at, emb:] = (piece - high.astype(f32)).astype(bf16)
        return carry

    lax.fori_loop(0, width // 256, weight_chunk, 0)
    started = []

    def send(src, dst, color, phase, slot, other):
        copy = remote(
            src, dst, send_sem.at[color, phase, slot], recv_sem.at[color, phase, slot], other
        )
        copy.start()
        started.append(copy)
        return copy

    def slab(axis, at, free):
        return tuple(at if a == axis else slice(None) for a in free)

    waiting = {}

    def swap_cores(k):
        low, high = CUTS[k]
        waiting[k] = [
            send(part.at[:, :, :, 1 - core, :, low:high], first[k], k, 0, 0, partner)
        ]

    def collect(k, phase):
        low, high = CUTS[k]
        for copy in waiting[k]:
            copy.wait_recv()
        if phase == 0:

            def add_first(i, carry):
                for x in range(4):
                    mine = part[i, x, :, core, :, low:high].astype(f32)
                    sums0[k][i, x] = (mine + first[k][i, x].astype(f32)).astype(bf16)
                return carry

            lax.fori_loop(0, 4, add_first, 0)
        else:
            before = ORDERS[k][phase - 1]
            free = [a for a in range(3) if a not in ORDERS[k][: phase - 1]]
            source = (sums0, sums1, sums2)[phase - 1][k]
            arrivals = (got1, got2, got3)[phase - 1][k]
            mine = source[slab(before, place[before], free)].astype(f32)
            for slot in range(3):
                mine = mine + arrivals[slot].astype(f32)
            if phase < 3:
                (sums1, sums2)[phase - 1][k][...] = mine.astype(bf16)
            else:
                total[:, low:high] = mine
        if phase < 3:
            axis = ORDERS[k][phase]
            left = [a for a in range(3) if a not in ORDERS[k][:phase]]
            waiting[k] = [
                send(
                    (sums0, sums1, sums2)[phase][k].at[
                        slab(axis, moved(place, axis, s)[axis], left)
                    ],
                    (got1, got2, got3)[phase][k].at[s - 1],
                    k,
                    1 + phase,
                    s - 1,
                    device_of(moved(place, axis, s), core),
                )
                for s in (1, 2, 3)
            ]

    def collect_bias(phase):
        for copy in waiting[BIAS]:
            copy.wait_recv()
        if phase == 0:
            bias_sum[0] = bias_part[...] + bias_got[0, 0]
        else:
            bias_sum[phase] = (bias_sum[phase - 1] + bias_got[phase, 0]) + (
                bias_got[phase, 1] + bias_got[phase, 2]
            )
        if phase < 3:
            waiting[BIAS] = [
                send(
                    bias_sum.at[phase],
                    bias_got.at[phase + 1, s - 1],
                    BIAS,
                    1 + phase,
                    s - 1,
                    device_of(moved(place, phase, s), core),
                )
                for s in (1, 2, 3)
            ]

    for k in range(3):
        swap_cores(k)
    waiting[BIAS] = [send(bias_part, bias_got.at[0, 0], BIAS, 0, 0, partner)]
    lax.fori_loop(0, width // 256, grad_chunk, 0)
    for k in range(3):
        collect(k, 0)
    collect_bias(0)

    def pick_grad(other, k):
        base = other * cap
        for j in range(cap):
            block[k, pl.ds(j, 1), :] = grad[pl.ds(inverse[0, base + j], 1), :]
        cold[other] = block[k].astype(bf16)

    def hot_tile(t, carry):
        mine = t * 256 + lax.broadcasted_iota(jnp.int32, (256, samples), 0)
        acc = jnp.zeros((256, 2 * emb), f32)
        for f in range(fields):
            mask = jnp.where(mine == ids[f : f + 1, :], 1.0, 0.0).astype(bf16)
            acc = acc + jnp.dot(
                mask, pair[f * samples : (f + 1) * samples, :], preferred_element_type=f32
            )
        both = (acc[:, :emb] + acc[:, emb:]).astype(bf16)
        x = pl.ds(lax.rem(t, 2) * 2, 2)
        part[t // 2, x, :, :, :, dense:] = both.reshape(2, 4, 2, 16, emb)
        return carry

    lax.fori_loop(0, hot_rows // 256, hot_tile, 0)
    swap_cores(3)
    keep.wait()
    all_cold = exchange(pick_grad, cold, returned, cold_send, cold_recv)
    collect(3, 0)
    for phase in (1, 2, 3):
        for k in range(COLORS):
            collect(k, phase)
        collect_bias(phase)
    bias_out[...] = bias_sum[3] * scale
    new = adam_update(master[...], m_in[...], v_in[...], total[:, :dense] * scale)[0]
    total_out[...] = total[:, :dense]
    out[place[0], place[1], place[2], core, :, :dense] = new.astype(bf16)
    out[place[0], place[1], place[2], core, :, dense:] = (total[:, dense:] * scale).astype(bf16)

    def update_cold():
        for load in loads[3:]:
            load.wait()
        all_cold.wait_recv()

        def widen(i, carry):
            wide[pl.ds(pl.multiple_of(i * cap, 8), cap), :] = returned[i].astype(f32)
            return carry

        lax.fori_loop(0, count, widen, 0)
        for j in range(cap):
            flat[j * count : (j + 1) * count, :] = wide[pl.ds(j, count, stride=cap), :].astype(
                bf16
            )

        def update_tile(t, carry):
            at = pl.ds(pl.multiple_of(t * 256, 256), 256)
            mine = t * 256 + lax.broadcasted_iota(jnp.int32, (256, 512), 0)
            acc = jnp.zeros((256, emb), f32)
            for c in range(count * cap // 512):
                cut = slice(c * 512, (c + 1) * 512)
                mask = jnp.where(mine == spread_rows[:, cut], 1.0, 0.0).astype(bf16)
                acc = acc + jnp.dot(mask, flat[cut, :], preferred_element_type=f32)
            new, m_new, v_new = adam_update(
                cold_table[at, :], cold_m[at, :], cold_v[at, :], acc * scale
            )
            cold_out[at, :] = new
            cold_m_out[at, :] = m_new
            cold_v_out[at, :] = v_new
            return carry

        lax.fori_loop(0, cold_table.shape[0] // 256, update_tile, 0)

    for phase in range(4):
        for k, (low, high) in enumerate(CUTS):
            order = ORDERS[k]
            for copy in waiting[k] if phase else []:
                copy.wait_recv()
            spread = order[3 - phase :]
            at = tuple(slice(None) if a in spread else place[a] for a in range(3))
            region = out.at[at + (core, slice(None), slice(low, high))]
            if phase < 3:
                axis = order[2 - phase]
                waiting[k] = [
                    send(
                        region, region, k, 4 + phase, s - 1, device_of(moved(place, axis, s), core)
                    )
                    for s in (1, 2, 3)
                ]
            else:
                waiting[k] = [send(region, region, k, 7, 0, partner)]
        if phase == 2:
            update_cold()
    for k in range(COLORS):
        for copy in waiting[k]:
            copy.wait_recv()
    for copy in started:
        copy.wait_send()
    for everything in (all_lists, all_stage, all_rows, all_cold):
        everything.wait_send()


def step_all(rows, lists, puts, ids, hot, cold_table, bias, dense_state, cot, down, up, cold_m, cold_v):
    f32, bf16, i32 = jnp.float32, jnp.bfloat16, jnp.int32
    count, cap = lists.shape
    hot_rows, emb = hot.shape
    samples, width = cot.shape
    lookups = samples * width // emb
    total_cols = 2 * down.shape[1] + emb
    widths = [high - low for low, high in CUTS]
    shapes = ((4, 4, 4), (4, 4, 4), (3, 4, 4), (4, 4), (3, 4), (4,), (3,))
    small = jax.ShapeDtypeStruct(dense_state[0].shape, f32)
    slab = jax.ShapeDtypeStruct(cold_table.shape, f32)
    vmem = pl.BlockSpec(memory_space=pltpu.VMEM)
    padded = jnp.pad(lists, ((0, 0), (0, emb - cap))).reshape(16, 8, 1, emb)
    return pl.pallas_call(
        step_kernel,
        out_shape=(
            jax.ShapeDtypeStruct((4, 4, 4, 2, 16, total_cols), bf16),
            jax.ShapeDtypeStruct(bias.shape, f32),
        )
        + (small,)
        + (slab,) * 3,
        in_specs=[pl.BlockSpec(memory_space=pltpu.SMEM)]
        + [vmem] * 9
        + [pl.BlockSpec(memory_space=pl.ANY)] * 5,
        out_specs=(vmem,) * 6,
        scratch_shapes=[
            pltpu.VMEM(shape + (16, cols), bf16) for shape in shapes for cols in widths
        ]
        + [
            pltpu.VMEM(cot.shape, bf16),
            pltpu.VMEM(down.shape, bf16),
            pltpu.VMEM(up.shape, bf16),
            pltpu.VMEM(cold_m.shape, f32),
            pltpu.VMEM(cold_v.shape, f32),
            pltpu.SMEM((16, 8, 1, emb), i32),
            pltpu.SMEM((1, count * cap), i32),
            pltpu.VMEM((16, 8, 1, emb), i32),
            pltpu.VMEM((count, cap, emb), bf16),
            pltpu.VMEM((count, cap, emb), bf16),
            pltpu.VMEM((8, cap, emb), f32),
            pltpu.VMEM((1, count * cap), i32),
            pltpu.VMEM((1, count * cap), i32),
            pltpu.VMEM((hot_rows + count * cap, emb), f32),
            pltpu.VMEM((samples, width), bf16),
            pltpu.VMEM((samples, width), bf16),
            pltpu.VMEM((lookups + 8, emb), f32),
            pltpu.VMEM((lookups, 2 * emb), bf16),
            pltpu.VMEM((4, 4, 4, 2, 16, total_cols), bf16),
            pltpu.VMEM(bias.shape, f32),
            pltpu.VMEM((count, cap, emb), bf16),
            pltpu.VMEM((count, cap, emb), bf16),
            pltpu.VMEM((count * cap + cap, emb), f32),
            pltpu.VMEM((count * cap, emb), bf16),
            pltpu.VMEM((16, total_cols), f32),
            pltpu.VMEM((4,) + bias.shape, f32),
            pltpu.VMEM((4, 3) + bias.shape, f32),
            pltpu.SemaphoreType.DMA((COLORS + 1, 8, 3)),
            pltpu.SemaphoreType.DMA((COLORS + 1, 8, 3)),
            pltpu.SemaphoreType.DMA((5,)),
        ]
        + [pltpu.SemaphoreType.DMA(())] * 7
        + [pltpu.VMEM((16, 8, 1, emb), i32)]
        + [pltpu.SemaphoreType.DMA(())] * 3,
        compiler_params=pltpu.CompilerParams(
            collective_id=0, has_side_effects=True, vmem_limit_bytes=48 * 2**20
        ),
        name="step_all",
    )(rows, padded, puts, ids, hot, cold_table, bias, *dense_state, cot, down, up, cold_m, cold_v)


def body(
    cotangent,
    hot_table,
    cold_table,
    cold_m,
    cold_v,
    cross_down,
    cross_up,
    cross_bias,
    dense_master,
    dense_m,
    dense_v,
    hot_ids,
    lookup_slot,
    fetch_rows,
):
    hot_rows = hot_table.shape[0]
    cross_width = cross_down.shape[0]
    is_hot = lookup_slot < 0
    lookup_rows = jnp.where(is_hot, hot_ids, hot_rows + lookup_slot).T.reshape(-1)
    hot_only = jnp.where(is_hot, hot_ids, -1).T
    gathered, bias_grad, total, cold_new, cold_m_new, cold_v_new = step_all(
        lookup_rows,
        fetch_rows[0],
        lookup_slot.T,
        hot_only,
        hot_table,
        cold_table,
        cross_bias.reshape(1, cross_width),
        (dense_master, dense_m, dense_v),
        cotangent,
        cross_down,
        cross_up,
        cold_m,
        cold_v,
    )
    flat = gathered.reshape(cross_width, -1)
    dense_cols = dense_master.shape[1]
    master_new, dense_m_new, dense_v_new = adam_update(
        dense_master, dense_m, dense_v, total * (1.0 / lax.axis_size("dev"))
    )
    hot_grad = flat[:, dense_cols:].astype(jnp.float32)
    bias_grad = bias_grad.reshape(cross_width)
    new_weights = flat[:, :dense_cols]
    return (
        hot_grad,
        bias_grad,
        cold_new,
        cold_m_new,
        cold_v_new,
        master_new,
        dense_m_new,
        dense_v_new,
        new_weights,
    )


def solution(mesh):
    return jax.shard_map(
        body,
        mesh=mesh,
        in_specs=(
            P("dev", None),
            P(),
            P("dev", None),
            P("dev", None),
            P("dev", None),
            P(),
            P(),
            P(),
            P("dev", None),
            P("dev", None),
            P("dev", None),
            P("dev", None),
            P("dev", None),
            P("dev", None, None),
        ),
        out_specs=(
            P(),
            P(),
            P("dev", None),
            P("dev", None),
            P("dev", None),
            P("dev", None),
            P("dev", None),
            P("dev", None),
            P(),
        ),
        check_vma=False,
    )
```

```python
import jax
import jax.numpy as jnp
from jax import lax
from jax.experimental import pallas as pl
from jax.experimental.pallas import tpu as pltpu
from jax.sharding import PartitionSpec as P

MESH = pl.DeviceIdType.MESH

first_decay = 0.9
second_decay = 0.999
adam_epsilon = 1e-08
learn_rate = 0.01
first_fix = 1.0 - (0.9**10) ** 10
second_fix = 1.0 - (0.999**10) ** 10


def adam_update(params, moment_one, moment_two, gradient):
    moment_one = first_decay * moment_one + (1.0 - first_decay) * gradient
    moment_two = second_decay * moment_two + (1.0 - second_decay) * gradient * gradient
    params = params - learn_rate * (moment_one / first_fix) / (
        jnp.sqrt(moment_two / second_fix) + adam_epsilon
    )
    return (params, moment_one, moment_two)

CUTS = ((0, 384), (384, 768), (768, 1024), (1024, 1152))
ORDERS = ((0, 1, 2), (1, 2, 0), (2, 0, 1), (2, 0, 1))
COLORS = len(CUTS)
BIAS = COLORS


def coords_of(me):
    return [me // 32, lax.rem(me // 8, 4), lax.rem(me // 2, 4)], lax.rem(me, 2)


def device_of(place, core):
    return place[0] * 32 + place[1] * 8 + place[2] * 2 + core


def moved(place, axis, step):
    return [lax.rem(p + step, 4) if a == axis else p for a, p in enumerate(place)]


def visit_peers(place, core, visit):
    tails = [lax.rem(place[2] + s, 4) * 2 + c for s in range(4) for c in (core, 1 - core)]

    def along_z(i, carry):
        z = lax.rem(place[0] + i, 4) * 32

        def along_x(j, inner):
            base = z + lax.rem(place[1] + j, 4) * 8
            visit([base + tail for tail in tails], i + j > 0)
            return inner

        return lax.fori_loop(0, 4, along_x, carry)

    lax.fori_loop(0, 4, along_z, 0)


def for_peers(place, core, act):
    def visit(others, away):
        pl.when(away)(lambda: act(others[0]))
        for other in others[1:]:
            act(other)

    visit_peers(place, core, visit)


def remote(source, target, send_sem, recv_sem, other):
    return pltpu.make_async_remote_copy(
        src_ref=source,
        dst_ref=target,
        send_sem=send_sem,
        recv_sem=recv_sem,
        device_id=(other,),
        device_id_type=MESH,
    )


def step_kernel(
    rows,
    lists,
    puts,
    ids,
    hot,
    cold_table,
    bias,
    master,
    m_in,
    v_in,
    cot_far,
    down_far,
    up_far,
    cold_m_far,
    cold_v_far,
    dense_out,
    hot_out,
    bias_out,
    total_out,
    cold_out,
    cold_m_out,
    cold_v_out,
    *rest,
):
    first, sums0, got1, sums1, got2, sums2, got3 = (
        rest[COLORS * i : COLORS * i + COLORS] for i in range(7)
    )
    rest = rest[COLORS * 7 - 21 :]
    cot, down, up, cold_m, cold_v, asked, inverse = rest[21:28]
    got, picked, arrived, block, spread_rows, inverse_row = rest[28:34]
    table, x_all, mix_all, grad, pair, part, bias_part = rest[34:41]
    cold, returned, wide, flat, total, bias_sum, bias_got = rest[41:48]
    mid = rest[58]
    stage_send, stage_recv, far_sem = rest[59:]
    send_sem, recv_sem, load_sem = rest[48:51]
    list_send, list_recv, row_send, row_recv, cold_send, cold_recv, own_sem = rest[51:58]
    f32, bf16 = jnp.float32, jnp.bfloat16
    me = lax.axis_index("dev")
    place, core = coords_of(me)
    partner = device_of(place, 1 - core)
    samples, width = cot.shape
    hot_rows, emb = hot.shape
    count, cap = picked.shape[:2]
    fields = width // emb
    half = down.shape[1]
    dense = 2 * half
    scale = 1.0 / count
    most = pl.ds(0, count - 1)
    nt = (((1,), (1,)), ((), ()))
    tn = (((0,), (0,)), ((), ()))

    plane, spot = place[0] * 4 + place[1], place[2] * 2 + core
    planes = [
        lax.rem(place[0] + i, 4) * 4 + lax.rem(place[1] + j, 4)
        for i in range(4)
        for j in range(4)
        if i + j > 0
    ]
    spots = [
        lax.rem(place[2] + i, 4) * 2 + c
        for i in range(4)
        for c in (core, 1 - core)
    ][1:]
    barrier = pltpu.get_barrier_semaphore()
    greeted = [other * 8 + spot for other in planes] + [plane * 8 + other for other in spots]
    for other in greeted:
        pl.semaphore_signal(barrier, inc=1, device_id=(other,), device_id_type=MESH)
    loads = [
        pltpu.make_async_copy(far, near, load_sem.at[i])
        for i, (far, near) in enumerate(
            (
                (cot_far, cot),
                (down_far, down),
                (up_far, up),
                (cold_m_far, cold_m),
                (cold_v_far, cold_v),
            )
        )
    ]
    for load in loads:
        load.start()

    which = lax.broadcasted_iota(jnp.int32, (8, samples), 0)
    sample = lax.broadcasted_iota(jnp.int32, (8, samples), 1).astype(f32)

    def invert(t, carry):
        mine = t * 256 + lax.broadcasted_iota(jnp.int32, (256, samples), 0)
        acc = jnp.zeros((8, 256), f32)
        for f in range(fields):
            mask = jnp.where(mine == puts[f : f + 1, :], 1.0, 0.0).astype(bf16)
            code = jnp.where(which == 0, f + 1.0, sample).astype(bf16)
            acc = acc + lax.dot_general(code, mask, nt, preferred_element_type=f32)
        found = ((acc[0:1] - 1.0) * samples + acc[1:2]).astype(jnp.int32)
        inverse_row[:, pl.ds(pl.multiple_of(t * 256, 256), 256)] = jnp.where(
            acc[0:1] > 0.5, jnp.clip(found, 0, fields * samples), fields * samples
        )
        return carry

    mid[plane] = lists[plane]
    pl.semaphore_wait(barrier, len(greeted))
    for other in planes:
        remote(lists.at[other], mid.at[plane], list_send, list_recv, other * 8 + spot).start()

    def widen_hot(i, carry):
        at = pl.ds(pl.multiple_of(i * 256, 256), 256)
        table[at, :] = hot[at, :].astype(f32)
        return carry

    lax.fori_loop(0, hot_rows // 256, widen_hot, 0)
    part_of = pl.ds(0, len(planes))
    all_lists = remote(lists.at[part_of], mid.at[part_of], list_send, list_recv, partner)
    all_lists.wait_recv()
    for other in spots:
        remote(
            mid.at[:, other], got.at[:, spot], stage_send, stage_recv, plane * 8 + other
        ).start()
    got[:, spot] = mid[:, spot]
    part_of = pl.ds(0, len(spots))
    all_stage = remote(mid.at[:, part_of], got.at[:, part_of], stage_send, stage_recv, partner)
    all_stage.wait_recv()
    turned = got[:, :, 0, :].reshape(count, emb).astype(f32).T.astype(jnp.int32)
    turned = jnp.clip(turned, 0, cold_table.shape[0] - 1)
    for j in range(cap):
        spread_rows[:, j * count : (j + 1) * count] = turned[j : j + 1, :]
    read = pltpu.make_async_copy(spread_rows, asked, far_sem)
    read.start()
    read.wait()

    def exchange(pick, source, target, sends, receives):
        def send(other):
            remote(source.at[other], target.at[me], sends, receives, other).start()

        def visit(others, away):
            for k, other in enumerate(others):
                pick(other, k)
            pl.when(away)(lambda: send(others[0]))
            for other in others[1:]:
                send(other)

        visit_peers(place, core, visit)
        target[me] = source[me]
        return remote(source.at[most], target.at[most], sends, receives, partner)

    def pick_row(other, k):
        for j in range(cap):
            block[k, pl.ds(j, 1), :] = cold_table[pl.ds(asked[0, j * count + other], 1), :]
        picked[other] = block[k].astype(bf16)

    all_rows = exchange(pick_row, picked, arrived, row_send, row_recv)
    lax.fori_loop(0, count * cap // 256, invert, 0)
    keep = pltpu.make_async_copy(inverse_row, inverse, own_sem)
    keep.start()
    grad[pl.ds(fields * samples, 8), :] = jnp.zeros((8, emb), f32)
    for load in loads[:3]:
        load.wait()
    all_rows.wait_recv()

    def widen_cold(i, carry):
        at = pl.ds(pl.multiple_of(hot_rows + i * cap, 8), cap)
        table[at, :] = arrived[i].astype(f32)
        return carry

    lax.fori_loop(0, count, widen_cold, 0)

    def gather_field(f, carry):
        cols = pl.ds(pl.multiple_of(f * emb, emb), emb)

        def gather_rows(i, inner):
            base = pl.multiple_of(f * samples + i * 16, 16)
            for j in range(16):
                grad[pl.ds(base + j, 1), :] = table[pl.ds(rows[base + j], 1), :]
            return inner

        lax.fori_loop(0, samples // 16, gather_rows, 0)
        x = grad[pl.ds(pl.multiple_of(f * samples, samples), samples), :]
        x_all[:, cols] = x.astype(bf16)
        mix_all[:, cols] = (cot[:, cols].astype(f32) * x).astype(bf16)
        return carry

    lax.fori_loop(0, fields, gather_field, 0)
    latent = jnp.dot(x_all[...], down[...], preferred_element_type=f32).astype(bf16)
    back = lax.dot_general(mix_all[...], up[...], nt, preferred_element_type=f32).astype(bf16)
    ones = jnp.ones((8, samples), bf16)

    def weight_chunk(n, carry):
        cols = pl.ds(pl.multiple_of(n * 256, 256), 256)
        z, x = n // 2, pl.ds(lax.rem(n, 2) * 2, 2)
        down_part = lax.dot_general(x_all[:, cols], back, tn, preferred_element_type=f32)
        up_part = lax.dot_general(mix_all[:, cols], latent, tn, preferred_element_type=f32)
        part[z, x, :, :, :, :half] = down_part.astype(bf16).reshape(2, 4, 2, 16, half)
        part[z, x, :, :, :, half:dense] = up_part.astype(bf16).reshape(2, 4, 2, 16, half)
        bias_part[:, cols] = jnp.dot(ones, mix_all[:, cols], preferred_element_type=f32)[:1]
        return carry

    def grad_chunk(n, carry):
        cols = pl.ds(pl.multiple_of(n * 256, 256), 256)
        mixing = jnp.dot(latent, up[:, cols], preferred_element_type=f32) + bias[:, cols]
        from_back = lax.dot_general(back, down[cols, :], nt, preferred_element_type=f32)
        g = cot[:, cols].astype(f32) * (mixing + 1.0) + from_back
        for h in range(2):
            at = pl.ds(pl.multiple_of((2 * n + h) * samples, samples), samples)
            piece = g[:, h * emb : (h + 1) * emb]
            grad[at, :] = piece
            high = piece.astype(bf16)
            pair[at, :emb] = high
            pair[at, emb:] = (piece - high.astype(f32)).astype(bf16)
        return carry

    lax.fori_loop(0, width // 256, weight_chunk, 0)
    started = []

    def send(src, dst, color, phase, slot, other):
        copy = remote(
            src, dst, send_sem.at[color, phase, slot], recv_sem.at[color, phase, slot], other
        )
        copy.start()
        started.append(copy)
        return copy

    def slab(axis, at, free):
        return tuple(at if a == axis else slice(None) for a in free)

    waiting = {}

    def swap_cores(k):
        low, high = CUTS[k]
        waiting[k] = [
            send(part.at[:, :, :, 1 - core, :, low:high], first[k], k, 0, 0, partner)
        ]

    def collect(k, phase):
        low, high = CUTS[k]
        for copy in waiting[k]:
            copy.wait_recv()
        if phase == 0:

            def add_first(i, carry):
                for x in range(4):
                    mine = part[i, x, :, core, :, low:high].astype(f32)
                    sums0[k][i, x] = (mine + first[k][i, x].astype(f32)).astype(bf16)
                return carry

            lax.fori_loop(0, 4, add_first, 0)
        else:
            before = ORDERS[k][phase - 1]
            free = [a for a in range(3) if a not in ORDERS[k][: phase - 1]]
            source = (sums0, sums1, sums2)[phase - 1][k]
            arrivals = (got1, got2, got3)[phase - 1][k]
            mine = source[slab(before, place[before], free)].astype(f32)
            for slot in range(3):
                mine = mine + arrivals[slot].astype(f32)
            if phase < 3:
                (sums1, sums2)[phase - 1][k][...] = mine.astype(bf16)
            else:
                total[:, low:high] = mine
        if phase < 3:
            axis = ORDERS[k][phase]
            left = [a for a in range(3) if a not in ORDERS[k][:phase]]
            waiting[k] = [
                send(
                    (sums0, sums1, sums2)[phase][k].at[
                        slab(axis, moved(place, axis, s)[axis], left)
                    ],
                    (got1, got2, got3)[phase][k].at[s - 1],
                    k,
                    1 + phase,
                    s - 1,
                    device_of(moved(place, axis, s), core),
                )
                for s in (1, 2, 3)
            ]

    def collect_bias(phase):
        for copy in waiting[BIAS]:
            copy.wait_recv()
        if phase == 0:
            bias_sum[0] = bias_part[...] + bias_got[0, 0]
        else:
            bias_sum[phase] = (bias_sum[phase - 1] + bias_got[phase, 0]) + (
                bias_got[phase, 1] + bias_got[phase, 2]
            )
        if phase < 3:
            waiting[BIAS] = [
                send(
                    bias_sum.at[phase],
                    bias_got.at[phase + 1, s - 1],
                    BIAS,
                    1 + phase,
                    s - 1,
                    device_of(moved(place, phase, s), core),
                )
                for s in (1, 2, 3)
            ]

    for k in range(3):
        swap_cores(k)
    waiting[BIAS] = [send(bias_part, bias_got.at[0, 0], BIAS, 0, 0, partner)]
    lax.fori_loop(0, width // 256, grad_chunk, 0)
    for k in range(3):
        collect(k, 0)
    collect_bias(0)

    def pick_grad(other, k):
        base = other * cap
        for j in range(cap):
            block[k, pl.ds(j, 1), :] = grad[pl.ds(inverse[0, base + j], 1), :]
        cold[other] = block[k].astype(bf16)

    def hot_tile(t, carry):
        mine = t * 256 + lax.broadcasted_iota(jnp.int32, (256, samples), 0)
        acc = jnp.zeros((256, 2 * emb), f32)
        for f in range(fields):
            mask = jnp.where(mine == ids[f : f + 1, :], 1.0, 0.0).astype(bf16)
            acc = acc + jnp.dot(
                mask, pair[f * samples : (f + 1) * samples, :], preferred_element_type=f32
            )
        both = (acc[:, :emb] + acc[:, emb:]).astype(bf16)
        x = pl.ds(lax.rem(t, 2) * 2, 2)
        part[t // 2, x, :, :, :, dense:] = both.reshape(2, 4, 2, 16, emb)
        return carry

    lax.fori_loop(0, hot_rows // 256, hot_tile, 0)
    swap_cores(3)
    keep.wait()
    all_cold = exchange(pick_grad, cold, returned, cold_send, cold_recv)
    collect(3, 0)
    for phase in (1, 2, 3):
        for k in range(COLORS):
            collect(k, phase)
        collect_bias(phase)
    bias_out[...] = bias_sum[3] * scale
    new = adam_update(master[...], m_in[...], v_in[...], total[:, :dense] * scale)[0]
    total_out[...] = total[:, :dense]
    at = (place[0], place[1], place[2], core)
    dense_out[at] = new.astype(bf16)
    hot_out[at] = (total[:, dense:] * scale).astype(bf16)

    def update_cold():
        for load in loads[3:]:
            load.wait()
        all_cold.wait_recv()

        def widen(i, carry):
            wide[pl.ds(pl.multiple_of(i * cap, 8), cap), :] = returned[i].astype(f32)
            return carry

        lax.fori_loop(0, count, widen, 0)
        for j in range(cap):
            flat[j * count : (j + 1) * count, :] = wide[pl.ds(j, count, stride=cap), :].astype(
                bf16
            )

        def update_tile(t, carry):
            at = pl.ds(pl.multiple_of(t * 256, 256), 256)
            mine = t * 256 + lax.broadcasted_iota(jnp.int32, (256, 512), 0)
            acc = jnp.zeros((256, emb), f32)
            for c in range(count * cap // 512):
                cut = slice(c * 512, (c + 1) * 512)
                mask = jnp.where(mine == spread_rows[:, cut], 1.0, 0.0).astype(bf16)
                acc = acc + jnp.dot(mask, flat[cut, :], preferred_element_type=f32)
            new, m_new, v_new = adam_update(
                cold_table[at, :], cold_m[at, :], cold_v[at, :], acc * scale
            )
            cold_out[at, :] = new
            cold_m_out[at, :] = m_new
            cold_v_out[at, :] = v_new
            return carry

        lax.fori_loop(0, cold_table.shape[0] // 256, update_tile, 0)

    for phase in range(4):
        for k, (low, high) in enumerate(CUTS):
            order = ORDERS[k]
            for copy in waiting[k] if phase else []:
                copy.wait_recv()
            spread = order[3 - phase :]
            at = tuple(slice(None) if a in spread else place[a] for a in range(3))
            at = at + (core, slice(None))
            region = dense_out.at[at + (slice(low, high),)] if high <= dense else hot_out.at[at]
            if phase < 3:
                axis = order[2 - phase]
                waiting[k] = [
                    send(
                        region, region, k, 4 + phase, s - 1, device_of(moved(place, axis, s), core)
                    )
                    for s in (1, 2, 3)
                ]
            else:
                waiting[k] = [send(region, region, k, 7, 0, partner)]
        if phase == 2:
            update_cold()
    for k in range(COLORS):
        for copy in waiting[k]:
            copy.wait_recv()
    for copy in started:
        copy.wait_send()
    for everything in (all_lists, all_stage, all_rows, all_cold):
        everything.wait_send()


def step_all(rows, lists, puts, ids, hot, cold_table, bias, dense_state, cot, down, up, cold_m, cold_v):
    f32, bf16, i32 = jnp.float32, jnp.bfloat16, jnp.int32
    count, cap = lists.shape
    hot_rows, emb = hot.shape
    samples, width = cot.shape
    lookups = samples * width // emb
    total_cols = 2 * down.shape[1] + emb
    widths = [high - low for low, high in CUTS]
    shapes = ((4, 4, 4), (4, 4, 4), (3, 4, 4), (4, 4), (3, 4), (4,), (3,))
    small = jax.ShapeDtypeStruct(dense_state[0].shape, f32)
    slab = jax.ShapeDtypeStruct(cold_table.shape, f32)
    vmem = pl.BlockSpec(memory_space=pltpu.VMEM)
    padded = jnp.pad(lists, ((0, 0), (0, emb - cap))).reshape(16, 8, 1, emb)
    return pl.pallas_call(
        step_kernel,
        out_shape=(
            jax.ShapeDtypeStruct((4, 4, 4, 2, 16, total_cols - emb), bf16),
            jax.ShapeDtypeStruct((4, 4, 4, 2, 16, emb), bf16),
            jax.ShapeDtypeStruct(bias.shape, f32),
        )
        + (small,)
        + (slab,) * 3,
        in_specs=[pl.BlockSpec(memory_space=pltpu.SMEM)]
        + [vmem] * 9
        + [pl.BlockSpec(memory_space=pl.ANY)] * 5,
        out_specs=(vmem,) * 7,
        scratch_shapes=[
            pltpu.VMEM(shape + (16, cols), bf16) for shape in shapes for cols in widths
        ]
        + [
            pltpu.VMEM(cot.shape, bf16),
            pltpu.VMEM(down.shape, bf16),
            pltpu.VMEM(up.shape, bf16),
            pltpu.VMEM(cold_m.shape, f32),
            pltpu.VMEM(cold_v.shape, f32),
            pltpu.SMEM((1, count * cap), i32),
            pltpu.SMEM((1, count * cap), i32),
            pltpu.VMEM((16, 8, 1, emb), i32),
            pltpu.VMEM((count, cap, emb), bf16),
            pltpu.VMEM((count, cap, emb), bf16),
            pltpu.VMEM((8, cap, emb), f32),
            pltpu.VMEM((1, count * cap), i32),
            pltpu.VMEM((1, count * cap), i32),
            pltpu.VMEM((hot_rows + count * cap, emb), f32),
            pltpu.VMEM((samples, width), bf16),
            pltpu.VMEM((samples, width), bf16),
            pltpu.VMEM((lookups + 8, emb), f32),
            pltpu.VMEM((lookups, 2 * emb), bf16),
            pltpu.VMEM((4, 4, 4, 2, 16, total_cols), bf16),
            pltpu.VMEM(bias.shape, f32),
            pltpu.VMEM((count, cap, emb), bf16),
            pltpu.VMEM((count, cap, emb), bf16),
            pltpu.VMEM((count * cap + cap, emb), f32),
            pltpu.VMEM((count * cap, emb), bf16),
            pltpu.VMEM((16, total_cols), f32),
            pltpu.VMEM((4,) + bias.shape, f32),
            pltpu.VMEM((4, 3) + bias.shape, f32),
            pltpu.SemaphoreType.DMA((COLORS + 1, 8, 3)),
            pltpu.SemaphoreType.DMA((COLORS + 1, 8, 3)),
            pltpu.SemaphoreType.DMA((5,)),
        ]
        + [pltpu.SemaphoreType.DMA(())] * 7
        + [pltpu.VMEM((16, 8, 1, emb), i32)]
        + [pltpu.SemaphoreType.DMA(())] * 3,
        compiler_params=pltpu.CompilerParams(
            collective_id=0, has_side_effects=True, vmem_limit_bytes=60 * 2**20
        ),
        name="step_all",
    )(rows, padded, puts, ids, hot, cold_table, bias, *dense_state, cot, down, up, cold_m, cold_v)


def body(
    cotangent,
    hot_table,
    cold_table,
    cold_m,
    cold_v,
    cross_down,
    cross_up,
    cross_bias,
    dense_master,
    dense_m,
    dense_v,
    hot_ids,
    lookup_slot,
    fetch_rows,
):
    hot_rows = hot_table.shape[0]
    cross_width = cross_down.shape[0]
    is_hot = lookup_slot < 0
    lookup_rows = jnp.where(is_hot, hot_ids, hot_rows + lookup_slot).T.reshape(-1)
    hot_only = jnp.where(is_hot, hot_ids, -1).T
    new_weights, hot_grad, bias_grad, total, cold_new, cold_m_new, cold_v_new = step_all(
        lookup_rows,
        fetch_rows[0],
        lookup_slot.T,
        hot_only,
        hot_table,
        cold_table,
        cross_bias.reshape(1, cross_width),
        (dense_master, dense_m, dense_v),
        cotangent,
        cross_down,
        cross_up,
        cold_m,
        cold_v,
    )
    master_new, dense_m_new, dense_v_new = adam_update(
        dense_master, dense_m, dense_v, total * (1.0 / lax.axis_size("dev"))
    )
    hot_grad = hot_grad.reshape(hot_table.shape).astype(jnp.float32)
    bias_grad = bias_grad.reshape(cross_width)
    new_weights = new_weights.reshape(cross_width, -1)
    return (
        hot_grad,
        bias_grad,
        cold_new,
        cold_m_new,
        cold_v_new,
        master_new,
        dense_m_new,
        dense_v_new,
        new_weights,
    )


def solution(mesh):
    return jax.shard_map(
        body,
        mesh=mesh,
        in_specs=(
            P("dev", None),
            P(),
            P("dev", None),
            P("dev", None),
            P("dev", None),
            P(),
            P(),
            P(),
            P("dev", None),
            P("dev", None),
            P("dev", None),
            P("dev", None),
            P("dev", None),
            P("dev", None, None),
        ),
        out_specs=(
            P(),
            P(),
            P("dev", None),
            P("dev", None),
            P("dev", None),
            P("dev", None),
            P("dev", None),
            P("dev", None),
            P(),
        ),
        check_vma=False,
    )
```

```python
import jax
import jax.numpy as jnp
from jax import lax
from jax.experimental import pallas as pl
from jax.experimental.pallas import tpu as pltpu
from jax.sharding import PartitionSpec as P

MESH = pl.DeviceIdType.MESH

first_decay = 0.9
second_decay = 0.999
adam_epsilon = 1e-08
learn_rate = 0.01
first_fix = 1.0 - (0.9**10) ** 10
second_fix = 1.0 - (0.999**10) ** 10


def adam_update(params, moment_one, moment_two, gradient):
    moment_one = first_decay * moment_one + (1.0 - first_decay) * gradient
    moment_two = second_decay * moment_two + (1.0 - second_decay) * gradient * gradient
    params = params - learn_rate * (moment_one / first_fix) / (
        jnp.sqrt(moment_two / second_fix) + adam_epsilon
    )
    return (params, moment_one, moment_two)

CUTS = ((0, 384), (384, 768), (768, 1024), (1024, 1152))
ORDERS = ((0, 1, 2), (1, 2, 0), (2, 0, 1), (2, 0, 1))
COLORS = len(CUTS)
BIAS = COLORS


def coords_of(me):
    return [me // 32, lax.rem(me // 8, 4), lax.rem(me // 2, 4)], lax.rem(me, 2)


def device_of(place, core):
    return place[0] * 32 + place[1] * 8 + place[2] * 2 + core


def moved(place, axis, step):
    return [lax.rem(p + step, 4) if a == axis else p for a, p in enumerate(place)]


def visit_peers(place, core, visit):
    tails = [lax.rem(place[2] + s, 4) * 2 + c for s in range(4) for c in (core, 1 - core)]

    def along_z(i, carry):
        z = lax.rem(place[0] + i, 4) * 32

        def along_x(j, inner):
            base = z + lax.rem(place[1] + j, 4) * 8
            visit([base + tail for tail in tails], i + j > 0)
            return inner

        return lax.fori_loop(0, 4, along_x, carry)

    lax.fori_loop(0, 4, along_z, 0)


def for_peers(place, core, act):
    def visit(others, away):
        pl.when(away)(lambda: act(others[0]))
        for other in others[1:]:
            act(other)

    visit_peers(place, core, visit)


def remote(source, target, send_sem, recv_sem, other):
    return pltpu.make_async_remote_copy(
        src_ref=source,
        dst_ref=target,
        send_sem=send_sem,
        recv_sem=recv_sem,
        device_id=(other,),
        device_id_type=MESH,
    )


def step_kernel(
    rows,
    lists,
    puts,
    ids,
    hot,
    cold_table,
    bias,
    master,
    m_in,
    v_in,
    cot_far,
    down_far,
    up_far,
    cold_m_far,
    cold_v_far,
    dense_out,
    hot_out,
    bias_out,
    total_out,
    cold_out,
    cold_m_out,
    cold_v_out,
    *rest,
):
    first, sums0, got1, sums1, got2, sums2, got3 = (
        rest[COLORS * i : COLORS * i + COLORS] for i in range(7)
    )
    rest = rest[COLORS * 7 - 21 :]
    cot, down, up, cold_m, cold_v, asked, inverse = rest[21:28]
    got, picked, arrived, block, spread_rows, inverse_row = rest[28:34]
    table, x_all, mix_all, grad, pair, part, bias_part = rest[34:41]
    cold, returned, wide, flat, total, bias_sum, bias_got = rest[41:48]
    mid = rest[58]
    stage_send, stage_recv, far_sem, turned_rows = rest[59:]
    send_sem, recv_sem, load_sem = rest[48:51]
    list_send, list_recv, row_send, row_recv, cold_send, cold_recv, own_sem = rest[51:58]
    f32, bf16 = jnp.float32, jnp.bfloat16
    me = lax.axis_index("dev")
    place, core = coords_of(me)
    partner = device_of(place, 1 - core)
    samples, width = cot.shape
    hot_rows, emb = hot.shape
    count, cap = picked.shape[:2]
    fields = width // emb
    half = down.shape[1]
    dense = 2 * half
    scale = 1.0 / count
    most = pl.ds(0, count - 1)
    nt = (((1,), (1,)), ((), ()))
    tn = (((0,), (0,)), ((), ()))

    plane, spot = place[0] * 4 + place[1], place[2] * 2 + core
    planes = [
        lax.rem(place[0] + i, 4) * 4 + lax.rem(place[1] + j, 4)
        for i in range(4)
        for j in range(4)
        if i + j > 0
    ]
    spots = [
        lax.rem(place[2] + i, 4) * 2 + c
        for i in range(4)
        for c in (core, 1 - core)
    ][1:]
    barrier = pltpu.get_barrier_semaphore()
    greeted = [other * 8 + spot for other in planes] + [plane * 8 + other for other in spots]
    for other in greeted:
        pl.semaphore_signal(barrier, inc=1, device_id=(other,), device_id_type=MESH)
    loads = [
        pltpu.make_async_copy(far, near, load_sem.at[i])
        for i, (far, near) in enumerate(
            (
                (cot_far, cot),
                (down_far, down),
                (up_far, up),
                (cold_m_far, cold_m),
                (cold_v_far, cold_v),
            )
        )
    ]
    for load in loads:
        load.start()

    which = lax.broadcasted_iota(jnp.int32, (8, samples), 0)
    sample = lax.broadcasted_iota(jnp.int32, (8, samples), 1).astype(f32)

    def invert(t, carry):
        mine = t * 256 + lax.broadcasted_iota(jnp.int32, (256, samples), 0)
        acc = jnp.zeros((8, 256), f32)
        for f in range(fields):
            mask = jnp.where(mine == puts[f : f + 1, :], 1.0, 0.0).astype(bf16)
            code = jnp.where(which == 0, f + 1.0, sample).astype(bf16)
            acc = acc + lax.dot_general(code, mask, nt, preferred_element_type=f32)
        found = ((acc[0:1] - 1.0) * samples + acc[1:2]).astype(jnp.int32)
        found = jnp.where(
            acc[0:1] > 0.5, jnp.clip(found, 0, fields * samples), fields * samples
        )
        inverse_row[pl.ds(2 * t, 1), :] = found[:, :count]
        inverse_row[pl.ds(2 * t + 1, 1), :] = found[:, count:]
        return carry

    mid[plane] = lists[plane]
    pl.semaphore_wait(barrier, len(greeted))
    for other in planes:
        remote(lists.at[other], mid.at[plane], list_send, list_recv, other * 8 + spot).start()

    def widen_hot(i, carry):
        at = pl.ds(pl.multiple_of(i * 256, 256), 256)
        table[at, :] = hot[at, :].astype(f32)
        return carry

    lax.fori_loop(0, hot_rows // 256, widen_hot, 0)
    part_of = pl.ds(0, len(planes))
    all_lists = remote(lists.at[part_of], mid.at[part_of], list_send, list_recv, partner)
    all_lists.wait_recv()
    for other in spots:
        remote(
            mid.at[:, other], got.at[:, spot], stage_send, stage_recv, plane * 8 + other
        ).start()
    got[:, spot] = mid[:, spot]
    part_of = pl.ds(0, len(spots))
    all_stage = remote(mid.at[:, part_of], got.at[:, part_of], stage_send, stage_recv, partner)
    all_stage.wait_recv()
    turned = got[:, :, 0, :].reshape(count, emb).astype(f32).T.astype(jnp.int32)
    turned = jnp.clip(turned, 0, cold_table.shape[0] - 1)
    for j in range(cap):
        spread_rows[:, j * count : (j + 1) * count] = turned[j : j + 1, :]
    turned_rows[...] = turned[:cap]
    read = pltpu.make_async_copy(turned_rows, asked, far_sem)
    read.start()
    read.wait()

    def exchange(pick, source, target, sends, receives):
        def send(other):
            remote(source.at[other], target.at[me], sends, receives, other).start()

        def visit(others, away):
            for k, other in enumerate(others):
                pick(other, k)
            pl.when(away)(lambda: send(others[0]))
            for other in others[1:]:
                send(other)

        visit_peers(place, core, visit)
        target[me] = source[me]
        return remote(source.at[most], target.at[most], sends, receives, partner)

    def pick_row(other, k):
        for j in range(cap):
            block[k, pl.ds(j, 1), :] = cold_table[pl.ds(asked[j, other], 1), :]
        picked[other] = block[k].astype(bf16)

    all_rows = exchange(pick_row, picked, arrived, row_send, row_recv)
    lax.fori_loop(0, count * cap // 256, invert, 0)
    keep = pltpu.make_async_copy(inverse_row, inverse, own_sem)
    keep.start()
    grad[pl.ds(fields * samples, 8), :] = jnp.zeros((8, emb), f32)
    for load in loads[:3]:
        load.wait()
    all_rows.wait_recv()

    def widen_cold(i, carry):
        at = pl.ds(pl.multiple_of(hot_rows + i * cap, 8), cap)
        table[at, :] = arrived[i].astype(f32)
        return carry

    lax.fori_loop(0, count, widen_cold, 0)

    def gather_field(f, carry):
        cols = pl.ds(pl.multiple_of(f * emb, emb), emb)

        def gather_rows(i, inner):
            base = pl.multiple_of(f * samples + i * 16, 16)
            for j in range(16):
                grad[pl.ds(base + j, 1), :] = table[pl.ds(rows[base + j], 1), :]
            return inner

        lax.fori_loop(0, samples // 16, gather_rows, 0)
        x = grad[pl.ds(pl.multiple_of(f * samples, samples), samples), :]
        x_all[:, cols] = x.astype(bf16)
        mix_all[:, cols] = (cot[:, cols].astype(f32) * x).astype(bf16)
        return carry

    lax.fori_loop(0, fields, gather_field, 0)
    latent = jnp.dot(x_all[...], down[...], preferred_element_type=f32).astype(bf16)
    back = lax.dot_general(mix_all[...], up[...], nt, preferred_element_type=f32).astype(bf16)
    ones = jnp.ones((8, samples), bf16)

    def weight_chunk(n, carry):
        cols = pl.ds(pl.multiple_of(n * 256, 256), 256)
        z, x = n // 2, pl.ds(lax.rem(n, 2) * 2, 2)
        down_part = lax.dot_general(x_all[:, cols], back, tn, preferred_element_type=f32)
        up_part = lax.dot_general(mix_all[:, cols], latent, tn, preferred_element_type=f32)
        part[z, x, :, :, :, :half] = down_part.astype(bf16).reshape(2, 4, 2, 16, half)
        part[z, x, :, :, :, half:dense] = up_part.astype(bf16).reshape(2, 4, 2, 16, half)
        bias_part[:, cols] = jnp.dot(ones, mix_all[:, cols], preferred_element_type=f32)[:1]
        return carry

    def grad_chunk(n, carry):
        cols = pl.ds(pl.multiple_of(n * 256, 256), 256)
        mixing = jnp.dot(latent, up[:, cols], preferred_element_type=f32) + bias[:, cols]
        from_back = lax.dot_general(back, down[cols, :], nt, preferred_element_type=f32)
        g = cot[:, cols].astype(f32) * (mixing + 1.0) + from_back
        for h in range(2):
            at = pl.ds(pl.multiple_of((2 * n + h) * samples, samples), samples)
            piece = g[:, h * emb : (h + 1) * emb]
            grad[at, :] = piece
            high = piece.astype(bf16)
            pair[at, :emb] = high
            pair[at, emb:] = (piece - high.astype(f32)).astype(bf16)
        return carry

    lax.fori_loop(0, width // 256, weight_chunk, 0)
    started = []

    def send(src, dst, color, phase, slot, other):
        copy = remote(
            src, dst, send_sem.at[color, phase, slot], recv_sem.at[color, phase, slot], other
        )
        copy.start()
        started.append(copy)
        return copy

    def slab(axis, at, free):
        return tuple(at if a == axis else slice(None) for a in free)

    waiting = {}

    def swap_cores(k):
        low, high = CUTS[k]
        waiting[k] = [
            send(part.at[:, :, :, 1 - core, :, low:high], first[k], k, 0, 0, partner)
        ]

    def collect(k, phase):
        low, high = CUTS[k]
        for copy in waiting[k]:
            copy.wait_recv()
        if phase == 0:

            def add_first(i, carry):
                for x in range(4):
                    mine = part[i, x, :, core, :, low:high].astype(f32)
                    sums0[k][i, x] = (mine + first[k][i, x].astype(f32)).astype(bf16)
                return carry

            lax.fori_loop(0, 4, add_first, 0)
        else:
            before = ORDERS[k][phase - 1]
            free = [a for a in range(3) if a not in ORDERS[k][: phase - 1]]
            source = (sums0, sums1, sums2)[phase - 1][k]
            arrivals = (got1, got2, got3)[phase - 1][k]
            mine = source[slab(before, place[before], free)].astype(f32)
            for slot in range(3):
                mine = mine + arrivals[slot].astype(f32)
            if phase < 3:
                (sums1, sums2)[phase - 1][k][...] = mine.astype(bf16)
            else:
                total[:, low:high] = mine
        if phase < 3:
            axis = ORDERS[k][phase]
            left = [a for a in range(3) if a not in ORDERS[k][:phase]]
            waiting[k] = [
                send(
                    (sums0, sums1, sums2)[phase][k].at[
                        slab(axis, moved(place, axis, s)[axis], left)
                    ],
                    (got1, got2, got3)[phase][k].at[s - 1],
                    k,
                    1 + phase,
                    s - 1,
                    device_of(moved(place, axis, s), core),
                )
                for s in (1, 2, 3)
            ]

    def collect_bias(phase):
        for copy in waiting[BIAS]:
            copy.wait_recv()
        if phase == 0:
            bias_sum[0] = bias_part[...] + bias_got[0, 0]
        else:
            bias_sum[phase] = (bias_sum[phase - 1] + bias_got[phase, 0]) + (
                bias_got[phase, 1] + bias_got[phase, 2]
            )
        if phase < 3:
            waiting[BIAS] = [
                send(
                    bias_sum.at[phase],
                    bias_got.at[phase + 1, s - 1],
                    BIAS,
                    1 + phase,
                    s - 1,
                    device_of(moved(place, phase, s), core),
                )
                for s in (1, 2, 3)
            ]

    for k in range(3):
        swap_cores(k)
    waiting[BIAS] = [send(bias_part, bias_got.at[0, 0], BIAS, 0, 0, partner)]
    lax.fori_loop(0, width // 256, grad_chunk, 0)
    for k in range(3):
        collect(k, 0)
    collect_bias(0)

    def pick_grad(other, k):
        for j in range(cap):
            block[k, pl.ds(j, 1), :] = grad[pl.ds(inverse[j, other], 1), :]
        cold[other] = block[k].astype(bf16)

    def hot_tile(t, carry):
        mine = t * 256 + lax.broadcasted_iota(jnp.int32, (256, samples), 0)
        acc = jnp.zeros((256, 2 * emb), f32)
        for f in range(fields):
            mask = jnp.where(mine == ids[f : f + 1, :], 1.0, 0.0).astype(bf16)
            acc = acc + jnp.dot(
                mask, pair[f * samples : (f + 1) * samples, :], preferred_element_type=f32
            )
        both = (acc[:, :emb] + acc[:, emb:]).astype(bf16)
        x = pl.ds(lax.rem(t, 2) * 2, 2)
        part[t // 2, x, :, :, :, dense:] = both.reshape(2, 4, 2, 16, emb)
        return carry

    lax.fori_loop(0, hot_rows // 256, hot_tile, 0)
    swap_cores(3)
    keep.wait()
    all_cold = exchange(pick_grad, cold, returned, cold_send, cold_recv)
    collect(3, 0)
    for phase in (1, 2, 3):
        for k in range(COLORS):
            collect(k, phase)
        collect_bias(phase)
    bias_out[...] = bias_sum[3] * scale
    new = adam_update(master[...], m_in[...], v_in[...], total[:, :dense] * scale)[0]
    total_out[...] = total[:, :dense]
    at = (place[0], place[1], place[2], core)
    dense_out[at] = new.astype(bf16)
    hot_out[at] = (total[:, dense:] * scale).astype(bf16)

    def update_cold():
        for load in loads[3:]:
            load.wait()
        all_cold.wait_recv()

        def widen(i, carry):
            wide[pl.ds(pl.multiple_of(i * cap, 8), cap), :] = returned[i].astype(f32)
            return carry

        lax.fori_loop(0, count, widen, 0)
        for j in range(cap):
            flat[j * count : (j + 1) * count, :] = wide[pl.ds(j, count, stride=cap), :].astype(
                bf16
            )

        def update_tile(t, carry):
            at = pl.ds(pl.multiple_of(t * 256, 256), 256)
            mine = t * 256 + lax.broadcasted_iota(jnp.int32, (256, 512), 0)
            acc = jnp.zeros((256, emb), f32)
            for c in range(count * cap // 512):
                cut = slice(c * 512, (c + 1) * 512)
                mask = jnp.where(mine == spread_rows[:, cut], 1.0, 0.0).astype(bf16)
                acc = acc + jnp.dot(mask, flat[cut, :], preferred_element_type=f32)
            new, m_new, v_new = adam_update(
                cold_table[at, :], cold_m[at, :], cold_v[at, :], acc * scale
            )
            cold_out[at, :] = new
            cold_m_out[at, :] = m_new
            cold_v_out[at, :] = v_new
            return carry

        lax.fori_loop(0, cold_table.shape[0] // 256, update_tile, 0)

    def region_of(k, spread, where):
        low, high = CUTS[k]
        at = tuple(slice(None) if a in spread else where[a] for a in range(3))
        at = at + (core, slice(None))
        return dense_out.at[at + (slice(low, high),)] if high <= dense else hot_out.at[at]

    for phase in range(3):
        for k in range(COLORS):
            for copy in waiting[k] if phase else []:
                copy.wait_recv()
            region = region_of(k, ORDERS[k][3 - phase :], place)
            axis = ORDERS[k][2 - phase]
            waiting[k] = [
                send(region, region, k, 4 + phase, s - 1, device_of(moved(place, axis, s), core))
                for s in (1, 2, 3)
            ]
            if phase == 2:
                crossing = [send(region, region, k, 0, 1, partner)]
                waiting[k] = (waiting[k], crossing)
    update_cold()
    for s in (1, 3, 2):
        for k in range(COLORS):
            waiting[k][0][s - 1].wait_recv()
            axis = ORDERS[k][0]
            region = region_of(k, ORDERS[k][1:], moved(place, axis, 4 - s))
            waiting[k][1].append(send(region, region, k, 7, s - 1, partner))
    for k in range(COLORS):
        for copy in waiting[k][1]:
            copy.wait_recv()
    for copy in started:
        copy.wait_send()
    for everything in (all_lists, all_stage, all_rows, all_cold):
        everything.wait_send()


def step_all(rows, lists, puts, ids, hot, cold_table, bias, dense_state, cot, down, up, cold_m, cold_v):
    f32, bf16, i32 = jnp.float32, jnp.bfloat16, jnp.int32
    count, cap = lists.shape
    hot_rows, emb = hot.shape
    samples, width = cot.shape
    lookups = samples * width // emb
    total_cols = 2 * down.shape[1] + emb
    widths = [high - low for low, high in CUTS]
    shapes = ((4, 4, 4), (4, 4, 4), (3, 4, 4), (4, 4), (3, 4), (4,), (3,))
    small = jax.ShapeDtypeStruct(dense_state[0].shape, f32)
    slab = jax.ShapeDtypeStruct(cold_table.shape, f32)
    vmem = pl.BlockSpec(memory_space=pltpu.VMEM)
    padded = jnp.pad(lists, ((0, 0), (0, emb - cap))).reshape(16, 8, 1, emb)
    return pl.pallas_call(
        step_kernel,
        out_shape=(
            jax.ShapeDtypeStruct((4, 4, 4, 2, 16, total_cols - emb), bf16),
            jax.ShapeDtypeStruct((4, 4, 4, 2, 16, emb), bf16),
            jax.ShapeDtypeStruct(bias.shape, f32),
        )
        + (small,)
        + (slab,) * 3,
        in_specs=[pl.BlockSpec(memory_space=pltpu.SMEM)]
        + [vmem] * 9
        + [pl.BlockSpec(memory_space=pl.ANY)] * 5,
        out_specs=(vmem,) * 7,
        scratch_shapes=[
            pltpu.VMEM(shape + (16, cols), bf16) for shape in shapes for cols in widths
        ]
        + [
            pltpu.VMEM(cot.shape, bf16),
            pltpu.VMEM(down.shape, bf16),
            pltpu.VMEM(up.shape, bf16),
            pltpu.VMEM(cold_m.shape, f32),
            pltpu.VMEM(cold_v.shape, f32),
            pltpu.SMEM((cap, count), i32),
            pltpu.SMEM((cap, count), i32),
            pltpu.VMEM((16, 8, 1, emb), i32),
            pltpu.VMEM((count, cap, emb), bf16),
            pltpu.VMEM((count, cap, emb), bf16),
            pltpu.VMEM((8, cap, emb), f32),
            pltpu.VMEM((1, count * cap), i32),
            pltpu.VMEM((cap, count), i32),
            pltpu.VMEM((hot_rows + count * cap, emb), f32),
            pltpu.VMEM((samples, width), bf16),
            pltpu.VMEM((samples, width), bf16),
            pltpu.VMEM((lookups + 8, emb), f32),
            pltpu.VMEM((lookups, 2 * emb), bf16),
            pltpu.VMEM((4, 4, 4, 2, 16, total_cols), bf16),
            pltpu.VMEM(bias.shape, f32),
            pltpu.VMEM((count, cap, emb), bf16),
            pltpu.VMEM((count, cap, emb), bf16),
            pltpu.VMEM((count * cap + cap, emb), f32),
            pltpu.VMEM((count * cap, emb), bf16),
            pltpu.VMEM((16, total_cols), f32),
            pltpu.VMEM((4,) + bias.shape, f32),
            pltpu.VMEM((4, 3) + bias.shape, f32),
            pltpu.SemaphoreType.DMA((COLORS + 1, 8, 3)),
            pltpu.SemaphoreType.DMA((COLORS + 1, 8, 3)),
            pltpu.SemaphoreType.DMA((5,)),
        ]
        + [pltpu.SemaphoreType.DMA(())] * 7
        + [pltpu.VMEM((16, 8, 1, emb), i32)]
        + [pltpu.SemaphoreType.DMA(())] * 3
        + [pltpu.VMEM((cap, count), i32)],
        compiler_params=pltpu.CompilerParams(
            collective_id=0, has_side_effects=True, vmem_limit_bytes=60 * 2**20
        ),
        name="step_all",
    )(rows, padded, puts, ids, hot, cold_table, bias, *dense_state, cot, down, up, cold_m, cold_v)


def body(
    cotangent,
    hot_table,
    cold_table,
    cold_m,
    cold_v,
    cross_down,
    cross_up,
    cross_bias,
    dense_master,
    dense_m,
    dense_v,
    hot_ids,
    lookup_slot,
    fetch_rows,
):
    owners, cap = fetch_rows.shape[1:]
    hot_rows = hot_table.shape[0]
    cross_width = cross_down.shape[0]
    is_hot = lookup_slot < 0
    lookup_rows = jnp.where(is_hot, hot_ids, hot_rows + lookup_slot).T.reshape(-1)
    hot_only = jnp.where(is_hot, hot_ids, -1).T
    new_weights, hot_grad, bias_grad, total, cold_new, cold_m_new, cold_v_new = step_all(
        lookup_rows,
        fetch_rows[0],
        jnp.where(is_hot, -1, lookup_slot % cap * owners + lookup_slot // cap).T,
        hot_only,
        hot_table,
        cold_table,
        cross_bias.reshape(1, cross_width),
        (dense_master, dense_m, dense_v),
        cotangent,
        cross_down,
        cross_up,
        cold_m,
        cold_v,
    )
    master_new, dense_m_new, dense_v_new = adam_update(
        dense_master, dense_m, dense_v, total * (1.0 / lax.axis_size("dev"))
    )
    hot_grad = hot_grad.reshape(hot_table.shape).astype(jnp.float32)
    bias_grad = bias_grad.reshape(cross_width)
    new_weights = new_weights.reshape(cross_width, -1)
    return (
        hot_grad,
        bias_grad,
        cold_new,
        cold_m_new,
        cold_v_new,
        master_new,
        dense_m_new,
        dense_v_new,
        new_weights,
    )


def solution(mesh):
    return jax.shard_map(
        body,
        mesh=mesh,
        in_specs=(
            P("dev", None),
            P(),
            P("dev", None),
            P("dev", None),
            P("dev", None),
            P(),
            P(),
            P(),
            P("dev", None),
            P("dev", None),
            P("dev", None),
            P("dev", None),
            P("dev", None),
            P("dev", None, None),
        ),
        out_specs=(
            P(),
            P(),
            P("dev", None),
            P("dev", None),
            P("dev", None),
            P("dev", None),
            P("dev", None),
            P("dev", None),
            P(),
        ),
        check_vma=False,
    )
```
